256 devices in a mesh: head: 8 (over y, x_hi), blk: 32 (over x_lo, z, core).
Axes of the slice: x: 4 (x_hi: 2, x_lo: 2; x = x_hi * 2 + x_lo), y: 4, z: 8, core: 2. Of those that a mesh axis runs over, the one named last changes fastest.
Arguments:
- queries: bfloat16 [32768, 2048], P(('blk', 'head')), may hold values from -10.5 to 10.5
- keys: bfloat16 [32768, 2048], P(('blk', 'head')), may hold values from -10.5 to 10.5
- values: bfloat16 [32768, 2048], P(('blk', 'head')), may hold values from -6 to 6
- d_out: bfloat16 [32768, 2048], P(('blk', 'head')), may hold values from -6 to 6
- saved_out: bfloat16 [32768, 2048], P(('blk', 'head')), may hold values from -3 to 3
- mask: int32 [256, 256], P('blk'), may hold values from 0 to 1, as said below
Outputs:
- d_queries: bfloat16 [32768, 2048], P(('blk', 'head'))
- d_keys: bfloat16 [32768, 2048], P(('blk', 'head'))
- d_values: bfloat16 [32768, 2048], P(('blk', 'head'))
The draws below stay inside these ranges and needn't reach their ends.
Inputs may be any that keep to these rules, and one draw needn't show every extreme that they name: mask[i, i] = 1. Tile i has grid position (i // 128, (i // 8) % 16, i % 8) in a grid of 2 x 16 x 8 tiles; mask[i, j] = 1 only where the positions of i and j differ by at most one along each of the three grid axes.
All inputs are finite; a program needn't handle non-finite values.
Results may differ from the reference program's by a relative error of at most 0.01.
Values may be sent and summed in bfloat16 or wider, within the bound.
No kernel may reach another device: no remote copies, remote signals or barrier semaphores. Data moves between devices by JAX's collectives and lax.ppermute only.
A program may use at most 192 MiB of HBM per device.

```python
import jax
import jax.numpy as jnp
from jax import lax

HEADS = 16
HEAD_DIM = 128
TILE = 128
TILE_T = 2
TOKENS = 32768
TILES = 256
TILE_W = 8
TILE_H = 16


def draw_queries(key, part):
    base = jax.random.truncated_normal(jax.random.fold_in(key, 1), -6.0, 6.0, (TOKENS, HEADS * HEAD_DIM), jnp.float32)
    return base.astype(jnp.bfloat16)


def draw_keys(key, part):
    base = jax.random.truncated_normal(jax.random.fold_in(key, 2), -6.0, 6.0, (TOKENS, HEADS * HEAD_DIM), jnp.float32)
    return base.astype(jnp.bfloat16)


def draw_mask(key, part):
    level_key, pair_key, tile_key = jax.random.split(jax.random.fold_in(key, 5), 3)
    group_count = TILE_T * TILE_H
    level = jax.random.randint(level_key, (group_count,), 1, 5)
    pair_draw = jax.random.randint(pair_key, (group_count, group_count), 0, 4)
    tile_draw = jax.random.randint(tile_key, (TILES, TILES), 0, 4)
    index = jnp.arange(TILES, dtype=jnp.int32)
    frame = index // (TILE_H * TILE_W)
    row_pos = index // TILE_W % TILE_H
    col_pos = index % TILE_W
    group_of = index // TILE_W
    near = (jnp.abs(frame[:, None] - frame[None, :]) <= 1) & (jnp.abs(row_pos[:, None] - row_pos[None, :]) <= 1) & (jnp.abs(col_pos[:, None] - col_pos[None, :]) <= 1)
    own_level = level[group_of][:, None]
    pair_keep = pair_draw[group_of][:, group_of] < own_level
    keep = near & pair_keep & (tile_draw <= own_level)
    keep = keep | (index[:, None] == index[None, :])
    return keep.astype(jnp.int32)


def shard_levels(stream_key, dims, pieces, least, high):
    def one(dim, shards_of):
        heights = jax.random.uniform(jax.random.fold_in(jax.random.fold_in(stream_key, 6), dim), (shards_of,), jnp.float32, least / len(pieces), high / len(pieces))
        return jnp.repeat(jnp.exp(heights), dims[dim] // shards_of).reshape((-1,) + (1,) * (len(dims) - dim - 1))

    factor_of = one(*pieces[0])
    for cut in pieces[1:]:
        factor_of = factor_of * one(*cut)
    return factor_of


def centred(key, shape, width, reach, cuts=(), kind=jnp.bfloat16):
    values = jax.random.normal(key, shape, jnp.float32) * width
    if len(cuts) > 0:
        values = shard_levels(key, shape, cuts, -0.22, 0.18) * values
    return jnp.clip(values, min=-reach, max=reach).astype(kind)


def setup_inputs(seed: int = 0) -> dict:
    splits = jax.random.split(jax.random.key(seed), 7)
    return {
        "queries": draw_queries(jax.random.fold_in(splits[6], 71), 0),
        "keys": draw_keys(jax.random.fold_in(splits[6], 71), 0),
        "values": centred(splits[2], (TOKENS, HEADS * HEAD_DIM), 1.0, 6.0, ((0, 256),)),
        "d_out": centred(splits[3], (TOKENS, HEADS * HEAD_DIM), 1.0, 6.0, ((0, 256),)),
        "saved_out": centred(splits[4], (TOKENS, HEADS * HEAD_DIM), 0.5, 3.0, ((0, 256),)),
        "mask": draw_mask(jax.random.fold_in(splits[6], 71), 0),
    }


masked_score = -1.0e30


def neighbours(index):
    plane = TILE_H * TILE_W
    frame = index // plane
    row_pos = (index // TILE_W) % TILE_H
    col_pos = index % TILE_W
    steps = jnp.arange(-1, 2, dtype=jnp.int32)
    frames = frame + steps[:, None, None]
    row_all = row_pos + steps[None, :, None]
    col_all = col_pos + steps[None, None, :]
    inside = (frames >= 0) & (frames < TILE_T) & (row_all >= 0) & (row_all < TILE_H) & (col_all >= 0) & (col_all < TILE_W)
    picked = (jnp.clip(frames, 0, TILE_T - 1) * TILE_H + jnp.clip(row_all, 0, TILE_H - 1)) * TILE_W + jnp.clip(col_all, 0, TILE_W - 1)
    return picked.reshape(9, 3).astype(jnp.int32), inside.reshape(9, 3)


def low_round(array):
    return lax.optimization_barrier(array.astype(jnp.bfloat16)).astype(jnp.float32)


def reference(queries, keys, values, d_out, saved_out, mask):
    scale = HEAD_DIM ** -0.5
    layout = (TILES, TILE, HEADS, HEAD_DIM)
    query_tiles = queries.reshape(layout)
    key_tiles = keys.reshape(layout)
    value_tiles = values.reshape(layout)
    grad_tiles = d_out.reshape(layout)
    output_tiles = saved_out.reshape(layout)

    def by_query(index):
        picked, inside = neighbours(index)
        picked = picked.reshape(-1)
        live = inside.reshape(-1) & (mask[index, picked] != 0)
        query_here = query_tiles[index].astype(jnp.float32)
        keys_near = key_tiles[picked].astype(jnp.float32)
        values_near = value_tiles[picked].astype(jnp.float32)
        grad_here = grad_tiles[index].astype(jnp.float32)
        output_here = output_tiles[index].astype(jnp.float32)
        scores = jnp.einsum("ihd,cjhd->hicj", query_here, keys_near) * scale
        scores = jnp.where(live[None, None, :, None], scores, masked_score)
        top = jnp.max(scores, axis=(2, 3))
        total = jnp.sum(jnp.exp(scores - top[:, :, None, None]), axis=(2, 3))
        lse = top + jnp.log(total)
        prob = jnp.exp(scores - lse[:, :, None, None])
        delta = jnp.einsum("ihd,ihd->hi", grad_here, output_here)
        dprob = jnp.einsum("ihd,cjhd->hicj", grad_here, values_near)
        dscore = low_round(prob * (dprob - delta[:, :, None, None]))
        query_grad = jnp.einsum("hicj,cjhd->ihd", dscore, keys_near) * scale
        return lse, delta, query_grad.astype(jnp.bfloat16)

    lse_all, delta_all, query_grads = lax.map(by_query, jnp.arange(TILES, dtype=jnp.int32))

    def by_key(index):
        picked, inside = neighbours(index)
        live = inside & (mask[picked, index] != 0)
        queries_near = query_tiles[picked].astype(jnp.float32)
        grads_near = grad_tiles[picked].astype(jnp.float32)
        lse_near = lse_all[picked]
        delta_near = delta_all[picked]
        key_here = key_tiles[index].astype(jnp.float32)
        value_here = value_tiles[index].astype(jnp.float32)
        scores = jnp.einsum("cwihd,jhd->cwhij", queries_near, key_here) * scale
        scores = jnp.where(live[:, :, None, None, None], scores, masked_score)
        prob = jnp.exp(scores - lse_near[..., None])
        prob_low = low_round(prob)
        dprob = jnp.einsum("cwihd,jhd->cwhij", grads_near, value_here)
        dscore = low_round(prob * (dprob - delta_near[..., None]))
        key_parts = jnp.einsum("cwhij,cwihd->cjhd", dscore, queries_near) * scale
        value_parts = jnp.einsum("cwhij,cwihd->cjhd", prob_low, grads_near)
        key_grad = jnp.sum(low_round(key_parts), axis=0)
        value_grad = jnp.sum(low_round(value_parts), axis=0)
        return key_grad.astype(jnp.bfloat16), value_grad.astype(jnp.bfloat16)

    key_grads, value_grads = lax.map(by_key, jnp.arange(TILES, dtype=jnp.int32))
    flat = (TOKENS, HEADS * HEAD_DIM)
    return query_grads.reshape(flat), key_grads.reshape(flat), value_grads.reshape(flat)
```

```python
import functools

import jax
import jax.numpy as jnp
from jax import lax
from jax.experimental import pallas as pl
from jax.experimental.pallas import tpu as pltpu
from jax.sharding import Mesh, PartitionSpec as P

HEADS = 16
DIM = 128
TILE = 128
COLS = 8
ROWS = 16
FRAMES = 2
GROUP = FRAMES * COLS
PAIRS = GROUP // 2
EXTRA = 16
BIG = 1e30
SCALE = DIM**-0.5
LOG2E = 1.4426950408889634
C = SCALE * LOG2E

F32 = jnp.float32
BF16 = jnp.bfloat16
VMEM_LIMIT = 58 * 1024 * 1024


def params(**kw):
    return pltpu.CompilerParams(vmem_limit_bytes=VMEM_LIMIT, **kw)


def pack_two_kernel(a_ref, b_ref, out_ref):
    for h in range(out_ref.shape[0]):
        out_ref[h, :TILE, :] = a_ref[:, h * DIM : (h + 1) * DIM]
        out_ref[h, TILE : 2 * TILE, :] = b_ref[:, h * DIM : (h + 1) * DIM]


def pack_two(a, b):
    step = 4
    block = pl.BlockSpec((TILE, step * DIM), lambda i: (0, i))
    return pl.pallas_call(
        pack_two_kernel,
        grid=(HEADS // step,),
        in_specs=[block, block],
        out_specs=pl.BlockSpec((step, 2 * TILE, DIM), lambda i: (i, 0, 0)),
        out_shape=jax.ShapeDtypeStruct((HEADS, 2 * TILE, DIM), BF16),
        compiler_params=params(),
        cost_estimate=pl.CostEstimate(flops=0, bytes_accessed=2**21, transcendentals=0),
        name="pack_keys_values",
    )(a, b)


def pack_queries_kernel(w_ref, q_ref, g_ref, o_ref, m_ref, out_ref):
    mine = m_ref[pl.ds(w_ref[0], 1), :].astype(F32)
    rows = lax.broadcasted_iota(jnp.int32, (EXTRA, TILE), 0)
    for h in range(out_ref.shape[0]):
        cols = slice(h * DIM, (h + 1) * DIM)
        q = q_ref[:, cols]
        g = g_ref[:, cols]
        out_ref[h, :TILE, :] = q
        out_ref[h, TILE : 2 * TILE, :] = g
        prod = g.astype(F32) * o_ref[:, cols].astype(F32)
        delta = jnp.sum(prod.T, axis=0, keepdims=True)
        high = delta.astype(BF16).astype(F32)
        low = delta - high
        extra = jnp.where(rows == 0, high, 0.0)
        extra = jnp.where(rows == 1, low, extra)
        extra = jnp.where(rows == 2, mine[:, :TILE], extra)
        extra = jnp.where(rows == 3, mine[:, TILE:], extra)
        out_ref[h, 2 * TILE :, :] = extra.astype(BF16)


def pack_queries(w, q, g, o, mask):
    step = 4
    block = pl.BlockSpec((TILE, step * DIM), lambda i: (0, i))
    return pl.pallas_call(
        pack_queries_kernel,
        grid=(HEADS // step,),
        in_specs=[
            pl.BlockSpec(memory_space=pltpu.SMEM),
            block,
            block,
            block,
            pl.BlockSpec((COLS, 2 * TILE), lambda i: (0, 0)),
        ],
        out_specs=pl.BlockSpec((step, 2 * TILE + EXTRA, DIM), lambda i: (i, 0, 0)),
        out_shape=jax.ShapeDtypeStruct((HEADS, 2 * TILE + EXTRA, DIM), BF16),
        compiler_params=params(),
        cost_estimate=pl.CostEstimate(flops=2**20, bytes_accessed=5 * 2**19, transcendentals=0),
        name="pack_queries",
    )(w, q, g, o, mask)


def unpack_kernel(in_ref, a_ref, b_ref):
    for h in range(in_ref.shape[0]):
        a_ref[:, h * DIM : (h + 1) * DIM] = in_ref[h, :TILE, :]
        b_ref[:, h * DIM : (h + 1) * DIM] = in_ref[h, TILE:, :]


def unpack_two(x):
    step = 4
    block = pl.BlockSpec((TILE, step * DIM), lambda i: (0, i))
    out = jax.ShapeDtypeStruct((TILE, HEADS * DIM), BF16)
    return pl.pallas_call(
        unpack_kernel,
        grid=(HEADS // step,),
        in_specs=[pl.BlockSpec((step, 2 * TILE, DIM), lambda i: (i, 0, 0))],
        out_specs=[block, block],
        out_shape=[out, out],
        compiler_params=params(),
        cost_estimate=pl.CostEstimate(flops=0, bytes_accessed=2**21, transcendentals=0),
        name="unpack_grads",
    )(x)


def dot_nt(a, b):
    return lax.dot_general(a, b, (((1,), (1,)), ((), ())), preferred_element_type=F32)


def dot_nn(a, b):
    return lax.dot_general(a, b, (((1,), (0,)), ((), ())), preferred_element_type=F32)


def key_tiles(wp, frame):
    found = []
    for step in (-1, 0, 1, 2):
        col = 2 * wp + step
        inside = (col >= 0) & (col < COLS)
        clamped = jnp.clip(col, 0, COLS - 1)
        found.append((frame * COLS + clamped, clamped, inside))
    return found


def penalty(rows_ref, m_ref, unit, tile, frame, col, inside):
    row = rows_ref[unit]
    live = (m_ref[tile, frame * TILE + row * COLS + col] != 0) & inside & (rows_ref[unit + 3] != 0)
    return jnp.where(live, 0.0, BIG).astype(F32)


def fold(x, op):
    return op(x.reshape(TILE // 8, 8, TILE), axis=0)


def query_side(qd_ref, t0):
    q = qd_ref[pl.ds(t0, 2), :TILE, :].reshape(2 * TILE, DIM)
    g = qd_ref[pl.ds(t0, 2), TILE : 2 * TILE, :].reshape(2 * TILE, DIM)
    delta = []
    for i in range(2):
        extra = qd_ref[t0 + i, 2 * TILE :, :].astype(F32)
        delta.append(extra[0:1, :] + extra[1:2, :])
    return q, g, jnp.concatenate(delta, axis=1)


SPANS = ((0, 1), (0, 2), (0, 2), (1, 2))


def unit_grads(rows_ref, m_ref, unit, kv_ref, kt_ref, dk_ref, dv_ref, scores, q, g, delta, lse, t0, wp, dqt):
    for frame in range(FRAMES):
        for j, (tile, col, inside) in enumerate(key_tiles(wp, frame)):
            lo, hi = SPANS[j]
            cut = slice(lo * TILE, hi * TILE)
            pens = [
                jnp.broadcast_to(penalty(rows_ref, m_ref, unit, t0 + i, frame, col, inside), (1, TILE))
                for i in range(lo, hi)
            ]
            level = lse[:, cut] + (jnp.concatenate(pens, axis=1) if len(pens) > 1 else pens[0])
            key = kv_ref[tile, :TILE, :]
            value = kv_ref[tile, TILE:, :]
            s = scores(frame, j) if scores is not None else dot_nt(key, q[cut])
            prob = jnp.exp2(s * C - level)
            dprob = dot_nt(value, g[cut])
            dscore = (prob * (dprob - delta[:, cut])).astype(BF16)
            prob = prob.astype(BF16)
            dv_ref[tile] += dot_nn(prob, g[cut])
            dk_ref[tile] += dot_nn(dscore, q[cut])
            part = dot_nn(kt_ref[tile], dscore)
            dqt[lo:hi] = [
                d + part[:, i * TILE : (i + 1) * TILE] for i, d in enumerate(dqt[lo:hi])
            ]
    return dqt


def stats_kernel(rows_ref, m_ref, qd_ref, own_ref, z_ref, c_ref, part_ref, lse_ref, dqt_ref, s_ref, kt_ref, dk_ref, dv_ref):
    dk_ref[...] = jnp.zeros_like(dk_ref)
    dv_ref[...] = jnp.zeros_like(dv_ref)

    def turn(t, carry):
        kt_ref[t] = z_ref[t, :TILE, :].T
        return carry

    lax.fori_loop(0, GROUP, turn, 0)

    def pair(p, carry):
        t0 = 2 * p
        wp = lax.rem(p, COLS // 2)
        q, g, delta = query_side(qd_ref, t0)
        top = [jnp.full((8, TILE), -BIG, F32) for _ in range(2)]
        pens = {}
        for unit, kv_ref in enumerate((z_ref, c_ref, own_ref)):
            for frame in range(FRAMES):
                for j, (tile, col, inside) in enumerate(key_tiles(wp, frame)):
                    lo, hi = SPANS[j]
                    s = dot_nt(kv_ref[tile, :TILE, :], q[lo * TILE : hi * TILE])
                    s_ref[unit, frame, j, :, lo * TILE : hi * TILE] = s
                    for i in range(lo, hi):
                        pen = penalty(rows_ref, m_ref, unit, t0 + i, frame, col, inside)
                        pens[unit, frame, j, i] = pen
                        piece = s[:, (i - lo) * TILE : (i - lo + 1) * TILE]
                        top[i] = jnp.maximum(top[i], fold(piece, jnp.max) - pen)
        lses = []
        for i in range(2):
            peak = jnp.max(top[i], axis=0, keepdims=True) * C
            total = jnp.zeros((8, TILE), F32)
            for unit in range(3):
                for frame in range(FRAMES):
                    for j in range(4):
                        if SPANS[j][0] <= i < SPANS[j][1]:
                            piece = s_ref[unit, frame, j, :, i * TILE : (i + 1) * TILE]
                            total += fold(jnp.exp2(piece * C - (peak + pens[unit, frame, j, i])), jnp.sum)
            lse = peak + jnp.log(jnp.sum(total, axis=0, keepdims=True)) * LOG2E
            lse_ref[t0 + i] = jnp.broadcast_to(lse, (8, TILE))
            lses.append(lse)
        lse = jnp.concatenate(lses, axis=1)

        def scores(frame, j):
            lo, hi = SPANS[j]
            return s_ref[0, frame, j, :, lo * TILE : hi * TILE]

        dqt = [jnp.zeros((DIM, TILE), F32) for _ in range(2)]
        dqt = unit_grads(rows_ref, m_ref, 0, z_ref, kt_ref, dk_ref, dv_ref, scores, q, g, delta, lse, t0, wp, dqt)
        dqt_ref[t0] = dqt[0]
        dqt_ref[t0 + 1] = dqt[1]
        return carry

    lax.fori_loop(0, PAIRS, pair, 0)
    part_ref[:, :TILE, :] = (dk_ref[...] * SCALE).astype(BF16)
    part_ref[:, TILE:, :] = dv_ref[...].astype(BF16)


def rest_kernel(
    rows_ref, m_ref, qd_ref, own_ref, c_ref, lse_ref, dqt_ref, part_ref, mine_ref, dq_ref,
    ktc_ref, kto_ref, dkc_ref, dvc_ref, dko_ref, dvo_ref,
):
    for ref in (dkc_ref, dvc_ref, dko_ref, dvo_ref):
        ref[...] = jnp.zeros_like(ref)

    def turn(t, carry):
        ktc_ref[t] = c_ref[t, :TILE, :].T
        kto_ref[t] = own_ref[t, :TILE, :].T
        return carry

    lax.fori_loop(0, GROUP, turn, 0)

    def pair(p, carry):
        t0 = 2 * p
        wp = lax.rem(p, COLS // 2)
        q, g, delta = query_side(qd_ref, t0)
        lse = jnp.concatenate([lse_ref[t0, 0:1, :], lse_ref[t0 + 1, 0:1, :]], axis=1)
        dqt = [dqt_ref[t0], dqt_ref[t0 + 1]]
        common = (None, q, g, delta, lse, t0, wp)
        dqt = unit_grads(rows_ref, m_ref, 1, c_ref, ktc_ref, dkc_ref, dvc_ref, *common, dqt)
        dqt = unit_grads(rows_ref, m_ref, 2, own_ref, kto_ref, dko_ref, dvo_ref, *common, dqt)
        for i in range(2):
            dq_ref[t0 + i] = (dqt[i].T * SCALE).astype(BF16)
        return carry

    lax.fori_loop(0, PAIRS, pair, 0)
    part_ref[:, :TILE, :] = (dkc_ref[...] * SCALE).astype(BF16)
    part_ref[:, TILE:, :] = dvc_ref[...].astype(BF16)
    mine_ref[:, :TILE, :] = dko_ref[...] * SCALE
    mine_ref[:, TILE:, :] = dvo_ref[...]


SMEM = pl.BlockSpec(memory_space=pltpu.SMEM)
VM = pl.BlockSpec(memory_space=pltpu.VMEM)


def acc():
    return pltpu.VMEM((GROUP, TILE, DIM), F32)


def turned():
    return pltpu.VMEM((GROUP, DIM, TILE), BF16)


def stats_and_far(rows, live, qd, own, far, near):
    return pl.pallas_call(
        stats_kernel,
        in_specs=[SMEM, SMEM, VM, VM, VM, VM],
        out_specs=[VM, VM, VM],
        out_shape=[
            jax.ShapeDtypeStruct((GROUP, 2 * TILE, DIM), BF16),
            jax.ShapeDtypeStruct((GROUP, 8, TILE), F32),
            jax.ShapeDtypeStruct((GROUP, DIM, TILE), F32),
        ],
        scratch_shapes=[
            pltpu.VMEM((3, FRAMES, 4, TILE, 2 * TILE), F32),
            turned(),
            acc(),
            acc(),
        ],
        compiler_params=params(),
        cost_estimate=pl.CostEstimate(flops=3 * 10**9, bytes_accessed=2**23, transcendentals=6 * 10**6),
        name="stats_and_far_row",
    )(rows, live, qd, own, far, near)


def rest(rows, live, qd, own, near, lse, dqt):
    return pl.pallas_call(
        rest_kernel,
        in_specs=[SMEM, SMEM, VM, VM, VM, VM, VM],
        out_specs=[VM, VM, VM],
        out_shape=[
            jax.ShapeDtypeStruct((GROUP, 2 * TILE, DIM), BF16),
            jax.ShapeDtypeStruct((GROUP, 2 * TILE, DIM), F32),
            jax.ShapeDtypeStruct((GROUP, TILE, DIM), BF16),
        ],
        scratch_shapes=[turned(), turned(), acc(), acc(), acc(), acc()],
        compiler_params=params(),
        cost_estimate=pl.CostEstimate(flops=4 * 10**9, bytes_accessed=2**23, transcendentals=3 * 10**6),
        name="near_and_own_rows",
    )(rows, live, qd, own, near, lse, dqt)


def per_device(queries, keys, values, d_out, saved_out, mask):
    group = ("frame", "head")
    row = lax.axis_index("row")
    even = lax.rem(row, 2) == 0
    chip_swap = [(i, i ^ 1) for i in range(ROWS)]
    link_swap = [(i, i + 1) for i in range(1, ROWS - 1, 2)] + [(i + 1, i) for i in range(1, ROWS - 1, 2)]

    def exchange(x):
        return lax.all_to_all(x, group, split_axis=0, concat_axis=0, tiled=True)

    own = exchange(pack_two(keys, values))
    w = lax.axis_index("head").astype(jnp.int32).reshape(1)
    qd = exchange(pack_queries(w, queries, d_out, saved_out, mask))
    far = lax.ppermute(own, "row", link_swap)
    near = lax.ppermute(own, "row", chip_swap)

    far_row = jnp.where(even, row - 1, row + 1)
    near_row = jnp.where(even, row + 1, row - 1)
    rows = jnp.stack([far_row, near_row, row]).astype(jnp.int32)
    inside = ((rows >= 0) & (rows < ROWS)).astype(jnp.int32)
    rows = jnp.concatenate([jnp.clip(rows, 0, ROWS - 1), inside])
    live = qd[:, 2 * TILE + 2 : 2 * TILE + 4, :].astype(jnp.int32).reshape(GROUP, 2 * TILE)

    far_part, lse, dqt = stats_and_far(rows, live, qd, own, far, near)
    far_back = lax.ppermute(far_part, "row", link_swap)
    near_part, mine, dq = rest(rows, live, qd, own, near, lse, dqt)
    near_back = lax.ppermute(near_part, "row", chip_swap)
    dq = exchange(dq)
    total = mine + near_back.astype(F32) + far_back.astype(F32)
    both = exchange(total.astype(BF16))
    d_keys, d_values = unpack_two(both)
    d_queries = dq.transpose(1, 0, 2).reshape(TILE, HEADS * DIM)
    return d_queries, d_keys, d_values


def solution(mesh):
    devices = mesh.devices
    if mesh.axis_names != ("head", "blk"):
        raise ValueError("mesh axes")
    heads = devices.shape[0]
    grid = Mesh(devices.reshape(heads, FRAMES, devices.shape[1] // FRAMES), ("head", "frame", "row"))
    tokens = P(("frame", "row", "head"), None)
    return jax.shard_map(
        per_device,
        mesh=grid,
        in_specs=(tokens,) * 5 + (P(("frame", "row"), None),),
        out_specs=(tokens,) * 3,
        check_vma=False,
    )
```

```python
import functools

import jax
import jax.numpy as jnp
from jax import lax
from jax.experimental import pallas as pl
from jax.experimental.pallas import tpu as pltpu
from jax.sharding import Mesh, PartitionSpec as P

HEADS = 16
DIM = 128
TILE = 128
COLS = 8
ROWS = 16
FRAMES = 2
GROUP = FRAMES * COLS
EXTRA = 16
FIRST = 3 * TILE + EXTRA
SECOND = TILE + EXTRA
BIG = 1e30
SCALE = DIM**-0.5
C = SCALE * 1.4426950408889634

F32 = jnp.float32
BF16 = jnp.bfloat16
VMEM_LIMIT = 20 * 1024 * 1024


def params(**kw):
    return pltpu.CompilerParams(vmem_limit_bytes=VMEM_LIMIT, **kw)


def small():
    return pltpu.CompilerParams(vmem_limit_bytes=8 * 1024 * 1024)


SMEM = pl.BlockSpec(memory_space=pltpu.SMEM)
VM = pl.BlockSpec(memory_space=pltpu.VMEM)
ANY = pl.BlockSpec(memory_space=pl.ANY)


CHUNKS = 4


def pack_first_kernel(w_ref, k_ref, v_ref, q_ref, m_ref, out_ref, buf_ref, mine_ref, in_sem, out_sem, mine_sem):
    wide = HEADS // CHUNKS * DIM
    refs = (k_ref, v_ref, q_ref)

    def fetch(part, i):
        cols = pl.ds(i * wide, wide)
        return pltpu.make_async_copy(refs[part].at[:, cols], buf_ref.at[part, :, cols], in_sem.at[part, i])

    def send(part, h):
        return pltpu.make_async_copy(
            buf_ref.at[part, :, pl.ds(h * DIM, DIM)], out_ref.at[h, pl.ds(part * TILE, TILE), :], out_sem.at[part, h]
        )

    def send_mask(h):
        return pltpu.make_async_copy(mine_ref, out_ref.at[h, pl.ds(3 * TILE, EXTRA), :], mine_sem.at[h])

    for i in range(CHUNKS):
        for part in range(3):
            fetch(part, i).start()
    mine = m_ref[pl.ds(w_ref[0], 1), :].astype(F32)
    rows = lax.broadcasted_iota(jnp.int32, (EXTRA, TILE), 0)
    extra = jnp.where(rows == 0, mine[:, :TILE], 0.0)
    mine_ref[...] = jnp.where(rows == 1, mine[:, TILE:], extra).astype(BF16)
    for i in range(CHUNKS):
        for part in range(3):
            fetch(part, i).wait()
            for h in range(i * HEADS // CHUNKS, (i + 1) * HEADS // CHUNKS):
                send(part, h).start()
    for h in range(HEADS):
        send_mask(h).start()
    for h in range(HEADS):
        for part in range(3):
            send(part, h).wait()
        send_mask(h).wait()


def pack_first(w, keys, values, queries, mask):
    return pl.pallas_call(
        pack_first_kernel,
        in_specs=[SMEM, ANY, ANY, ANY, VM],
        out_specs=ANY,
        out_shape=jax.ShapeDtypeStruct((HEADS, FIRST, DIM), BF16),
        scratch_shapes=[
            pltpu.VMEM((3, TILE, HEADS * DIM), BF16),
            pltpu.VMEM((EXTRA, TILE), BF16),
            pltpu.SemaphoreType.DMA((3, CHUNKS)),
            pltpu.SemaphoreType.DMA((3, HEADS)),
            pltpu.SemaphoreType.DMA((HEADS,)),
        ],
        compiler_params=pltpu.CompilerParams(vmem_limit_bytes=58 * 1024 * 1024),
        cost_estimate=pl.CostEstimate(flops=0, bytes_accessed=3 * 2**20, transcendentals=0),
        name="pack_first",
    )(w, keys, values, queries, mask)


def pack_second_kernel(g_ref, o_ref, out_ref):
    rows = lax.broadcasted_iota(jnp.int32, (EXTRA, TILE), 0)
    for h in range(out_ref.shape[0]):
        cols = slice(h * DIM, (h + 1) * DIM)
        g = g_ref[:, cols]
        out_ref[h, :TILE, :] = g
        prod = g.astype(F32) * o_ref[:, cols].astype(F32)
        delta = jnp.sum(prod.T, axis=0, keepdims=True)
        high = delta.astype(BF16).astype(F32)
        extra = jnp.where(rows == 0, high, 0.0)
        out_ref[h, TILE:, :] = jnp.where(rows == 1, delta - high, extra).astype(BF16)


def pack_second(g, o):
    step = 4
    block = pl.BlockSpec((TILE, step * DIM), lambda i: (0, i))
    return pl.pallas_call(
        pack_second_kernel,
        grid=(HEADS // step,),
        in_specs=[block, block],
        out_specs=pl.BlockSpec((step, SECOND, DIM), lambda i: (i, 0, 0)),
        out_shape=jax.ShapeDtypeStruct((HEADS, SECOND, DIM), BF16),
        compiler_params=small(),
        cost_estimate=pl.CostEstimate(flops=2**20, bytes_accessed=3 * 2**19, transcendentals=0),
        name="pack_second",
    )(g, o)


def unpack_kernel(in_ref, q_ref, k_ref, v_ref, sem):
    refs = (q_ref, k_ref, v_ref)

    def move(part, h):
        return pltpu.make_async_copy(
            in_ref.at[h, pl.ds(part * TILE, TILE), :], refs[part].at[:, pl.ds(h * DIM, DIM)], sem.at[part, h]
        )

    for h in range(HEADS):
        for part in range(3):
            move(part, h).start()
    for h in range(HEADS):
        for part in range(3):
            move(part, h).wait()


def unpack(x):
    out = jax.ShapeDtypeStruct((TILE, HEADS * DIM), BF16)
    return pl.pallas_call(
        unpack_kernel,
        in_specs=[VM],
        out_specs=[ANY] * 3,
        out_shape=[out] * 3,
        scratch_shapes=[pltpu.SemaphoreType.DMA((3, HEADS))],
        compiler_params=small(),
        cost_estimate=pl.CostEstimate(flops=0, bytes_accessed=3 * 2**20, transcendentals=0),
        name="unpack_grads",
    )(x)


def add_kernel(mine_ref, near_ref, far_ref, out_ref):
    out_ref[:, :TILE, :] = mine_ref[:, :TILE, :]
    total = mine_ref[:, TILE:, :].astype(F32) + near_ref[...].astype(F32) + far_ref[...].astype(F32)
    out_ref[:, TILE:, :] = total.astype(BF16)


def add_parts(mine, near, far):
    step = 4
    block = pl.BlockSpec((step, 2 * TILE, DIM), lambda i: (i, 0, 0))
    wide = pl.BlockSpec((step, 3 * TILE, DIM), lambda i: (i, 0, 0))
    return pl.pallas_call(
        add_kernel,
        grid=(GROUP // step,),
        in_specs=[wide, block, block],
        out_specs=wide,
        out_shape=jax.ShapeDtypeStruct((GROUP, 3 * TILE, DIM), BF16),
        compiler_params=small(),
        cost_estimate=pl.CostEstimate(flops=2**20, bytes_accessed=5 * 2**20, transcendentals=0),
        name="add_parts",
    )(mine, near, far)


def dot_nt(a, b):
    return lax.dot_general(a, b, (((1,), (1,)), ((), ())), preferred_element_type=F32)


def dot_nn(a, b):
    return lax.dot_general(a, b, (((1,), (0,)), ((), ())), preferred_element_type=F32)


def sweep(body):
    edge = COLS - 1
    body(0, ((1, 0, True, False), (2, 1, True, False)))

    def inner(w, carry):
        body(w, ((0, w - 1, False, True), (1, w, False, False), (2, w + 1, True, False)))
        return carry

    lax.fori_loop(1, edge, inner, 0)
    body(edge, ((0, edge - 1, False, True), (1, edge, False, True)))


def both(ref, col, part):
    rows = slice(part * TILE, (part + 1) * TILE)
    return jnp.concatenate([ref[col, rows, :], ref[COLS + col, rows, :]], axis=0)


def penalties(rows_ref, m_ref, unit, w, col):
    found = []
    inside = rows_ref[unit + 3] != 0
    for key_frame in range(FRAMES):
        at = key_frame * TILE + rows_ref[unit] * COLS + col
        cells = []
        for frame in range(FRAMES):
            live = (m_ref[frame * COLS + w, at] != 0) & inside
            cells.append(jnp.broadcast_to(jnp.where(live, 0.0, BIG).astype(F32), (1, TILE)))
        found.append(jnp.concatenate(cells, axis=1))
    return found


def fold(x, op):
    return op(x.reshape(TILE // 8, 8, 2 * TILE), axis=0)


def grad_side(gd_ref, w):
    g = both(gd_ref, w, 0)
    delta = []
    for frame in range(FRAMES):
        extra = gd_ref[frame * COLS + w, TILE:, :].astype(F32)
        delta.append(extra[0:1, :] + extra[1:2, :])
    return g, jnp.concatenate(delta, axis=1)


def step_grads(kv_ref, kt_ref, dk_ref, dv_ref, out_ref, at, prob, q, g, delta, col, first, last):
    dprob = dot_nt(both(kv_ref, col, 1), g)
    dscore = (prob * (dprob - delta)).astype(BF16)
    prob = prob.astype(BF16)
    dv = dot_nn(prob, g)
    dk = dot_nn(dscore, q)
    if first:
        turned_keys = jnp.concatenate([kv_ref[col, :TILE, :].T, kv_ref[COLS + col, :TILE, :].T], axis=1)
        kt_ref[col] = turned_keys
    else:
        turned_keys = kt_ref[col]
    for frame in range(FRAMES):
        rows = slice(frame * TILE, (frame + 1) * TILE)
        tile = frame * COLS + col
        dv_here, dk_here = dv[rows], dk[rows]
        if not first:
            dv_here += dv_ref[tile]
            dk_here += dk_ref[tile]
        if last:
            out_ref[tile, at * TILE : (at + 1) * TILE, :] = (dk_here * SCALE).astype(BF16)
            out_ref[tile, (at + 1) * TILE : (at + 2) * TILE, :] = dv_here.astype(BF16)
        else:
            dv_ref[tile] = dv_here
            dk_ref[tile] = dk_here
    return dot_nn(turned_keys, dscore)


def halves(x):
    return [x[:TILE], x[TILE:]]


def early_kernel(rows_ref, m_ref, first_ref, near_ref, e_ref, peak_ref, total_ref, s_ref):
    units = ((0, near_ref), (1, first_ref))

    def body(w, steps):
        q = both(first_ref, w, 2)
        top = jnp.full((8, 2 * TILE), -BIG, F32)
        pens = {}
        for unit, kv_ref in units:
            for place, col, _, _ in steps:
                s = dot_nt(both(kv_ref, col, 0), q)
                s_ref[unit, place] = s
                pens[unit, place] = penalties(rows_ref, m_ref, unit, w, col)
                for piece, pen in zip(halves(s), pens[unit, place]):
                    top = jnp.maximum(top, fold(piece, jnp.max) - pen)
        peak = jnp.max(top, axis=0, keepdims=True)
        total = jnp.zeros((8, 2 * TILE), F32)
        for unit, _ in units:
            for place, _, _, _ in steps:
                for frame in range(FRAMES):
                    rows = slice(frame * TILE, (frame + 1) * TILE)
                    e = jnp.exp2(s_ref[unit, place, rows, :] * C - (peak * C + pens[unit, place][frame]))
                    e_ref[w, unit, place, rows, :] = e.astype(BF16)
                    total += fold(e, jnp.sum)
        peak_ref[w] = jnp.broadcast_to(peak, (8, 2 * TILE))
        total_ref[w] = jnp.broadcast_to(jnp.sum(total, axis=0, keepdims=True), (8, 2 * TILE))

    sweep(body)


def far_kernel(
    rows_ref, m_ref, first_ref, gd_ref, far_ref, peak_ref, total_ref, part_ref, share_ref, dqt_ref,
    s_ref, kt_ref, dk_ref, dv_ref,
):
    def body(w, steps):
        q = both(first_ref, w, 2)
        g, delta = grad_side(gd_ref, w)
        early = peak_ref[w]
        top = early
        pens = {}
        for place, col, _, _ in steps:
            s = dot_nt(both(far_ref, col, 0), q)
            s_ref[place] = s
            pens[place] = penalties(rows_ref, m_ref, 2, w, col)
            for piece, pen in zip(halves(s), pens[place]):
                top = jnp.maximum(top, fold(piece, jnp.max) - pen)
        peak = jnp.max(top, axis=0, keepdims=True)
        total = jnp.zeros((8, 2 * TILE), F32)
        for place, _, _, _ in steps:
            for frame in range(FRAMES):
                rows = slice(frame * TILE, (frame + 1) * TILE)
                e = jnp.exp2(s_ref[place, rows, :] * C - (peak * C + pens[place][frame]))
                s_ref[place, rows, :] = e
                total += fold(e, jnp.sum)
        shrink = jnp.exp2((early[0:1, :] - peak) * C)
        share = 1.0 / (jnp.sum(total, axis=0, keepdims=True) + total_ref[w, 0:1, :] * shrink)
        share_ref[w] = jnp.broadcast_to(shrink * share, (8, 2 * TILE))
        dqt = jnp.zeros((DIM, 2 * TILE), F32)
        for place, col, first, last in steps:
            prob = s_ref[place] * share
            dqt += step_grads(far_ref, kt_ref, dk_ref, dv_ref, part_ref, 0, prob, q, g, delta, col, first, last)
        dqt_ref[w] = dqt

    sweep(body)


def rest_kernel(
    first_ref, gd_ref, near_ref, e_ref, share_ref, dqt_ref, part_ref, mine_ref,
    ktc_ref, kto_ref, dkc_ref, dvc_ref, dko_ref, dvo_ref,
):
    def body(w, steps):
        q = both(first_ref, w, 2)
        g, delta = grad_side(gd_ref, w)
        share = share_ref[w, 0:1, :]
        dqt = dqt_ref[w]
        for place, col, first, last in steps:
            prob = e_ref[w, 0, place].astype(F32) * share
            dqt += step_grads(near_ref, ktc_ref, dkc_ref, dvc_ref, part_ref, 0, prob, q, g, delta, col, first, last)
            prob = e_ref[w, 1, place].astype(F32) * share
            dqt += step_grads(first_ref, kto_ref, dko_ref, dvo_ref, mine_ref, 1, prob, q, g, delta, col, first, last)
        dq = (dqt.T * SCALE).astype(BF16)
        mine_ref[w, :TILE, :] = dq[:TILE]
        mine_ref[COLS + w, :TILE, :] = dq[TILE:]

    sweep(body)


def acc():
    return pltpu.VMEM((GROUP, TILE, DIM), F32)


def turned():
    return pltpu.VMEM((COLS, DIM, 2 * TILE), BF16)


ROWS_OF = jax.ShapeDtypeStruct((COLS, 8, 2 * TILE), F32)
PART = jax.ShapeDtypeStruct((GROUP, 2 * TILE, DIM), BF16)


def early(rows, live, first, near):
    return pl.pallas_call(
        early_kernel,
        in_specs=[SMEM, SMEM, VM, VM],
        out_specs=[VM, VM, VM],
        out_shape=[jax.ShapeDtypeStruct((COLS, 2, 3, 2 * TILE, 2 * TILE), BF16), ROWS_OF, ROWS_OF],
        scratch_shapes=[pltpu.VMEM((2, 3, 2 * TILE, 2 * TILE), F32)],
        compiler_params=params(),
        cost_estimate=pl.CostEstimate(flops=2 * 10**9, bytes_accessed=3 * 2**20, transcendentals=3 * 10**6),
        name="near_and_own_scores",
    )(rows, live, first, near)


def far_row(rows, live, first, gd, far, peak, total):
    return pl.pallas_call(
        far_kernel,
        in_specs=[SMEM, SMEM, VM, VM, VM, VM, VM],
        out_specs=[VM, VM, VM],
        out_shape=[PART, ROWS_OF, jax.ShapeDtypeStruct((COLS, DIM, 2 * TILE), F32)],
        scratch_shapes=[pltpu.VMEM((3, 2 * TILE, 2 * TILE), F32), turned(), acc(), acc()],
        compiler_params=params(),
        cost_estimate=pl.CostEstimate(flops=2 * 10**9, bytes_accessed=2**22, transcendentals=2 * 10**6),
        name="far_row",
    )(rows, live, first, gd, far, peak, total)


def rest(first, gd, near, e, share, dqt):
    return pl.pallas_call(
        rest_kernel,
        in_specs=[VM] * 6,
        out_specs=[VM, VM],
        out_shape=[PART, jax.ShapeDtypeStruct((GROUP, 3 * TILE, DIM), BF16)],
        scratch_shapes=[turned(), turned(), acc(), acc(), acc(), acc()],
        compiler_params=params(),
        cost_estimate=pl.CostEstimate(flops=4 * 10**9, bytes_accessed=2**23, transcendentals=0),
        name="near_and_own_rows",
    )(first, gd, near, e, share, dqt)


def per_device(queries, keys, values, d_out, saved_out, mask):
    group = ("frame", "head")
    row = lax.axis_index("row")
    is_even = lax.rem(row, 2) == 0
    chip_swap = [(i, i ^ 1) for i in range(ROWS)]
    link_swap = [(i, i + 1) for i in range(1, ROWS - 1, 2)] + [(i + 1, i) for i in range(1, ROWS - 1, 2)]

    def exchange(x):
        return lax.all_to_all(x, group, split_axis=0, concat_axis=0, tiled=True)

    w = lax.axis_index("head").astype(jnp.int32).reshape(1)
    first = exchange(pack_first(w, keys, values, queries, mask))
    second = pack_second(d_out, saved_out)
    first, second = lax.optimization_barrier((first, second))
    own = first[:, : 2 * TILE, :]
    far = lax.ppermute(own, "row", link_swap)
    near = lax.ppermute(own, "row", chip_swap)
    gd = exchange(second)

    far_index = jnp.where(is_even, row - 1, row + 1)
    near_index = jnp.where(is_even, row + 1, row - 1)
    rows = jnp.stack([near_index, row, far_index]).astype(jnp.int32)
    inside = ((rows >= 0) & (rows < ROWS)).astype(jnp.int32)
    rows = jnp.concatenate([jnp.clip(rows, 0, ROWS - 1), inside])
    live = first[:, 3 * TILE : 3 * TILE + 2, :].astype(jnp.int32).reshape(GROUP, 2 * TILE)

    e, peak, total = early(rows, live, first, near)
    far_part, share, dqt = far_row(rows, live, first, gd, far, peak, total)
    far_back = lax.ppermute(far_part, "row", link_swap)
    near_part, mine = rest(first, gd, near, e, share, dqt)
    far_back, mine = lax.optimization_barrier((far_back, mine))
    near_back = lax.ppermute(near_part, "row", chip_swap)
    return tuple(unpack(exchange(add_parts(mine, near_back, far_back))))


def solution(mesh):
    devices = mesh.devices
    if mesh.axis_names != ("head", "blk"):
        raise ValueError("mesh axes")
    heads = devices.shape[0]
    grid = Mesh(devices.reshape(heads, FRAMES, devices.shape[1] // FRAMES), ("head", "frame", "row"))
    tokens = P(("frame", "row", "head"), None)
    return jax.shard_map(
        per_device,
        mesh=grid,
        in_specs=(tokens,) * 5 + (P(("frame", "row"), None),),
        out_specs=(tokens,) * 3,
        check_vma=False,
    )
```

```python
import functools

import jax
import jax.numpy as jnp
from jax import lax
from jax.experimental import pallas as pl
from jax.experimental.pallas import tpu as pltpu
from jax.sharding import Mesh, PartitionSpec as P

HEADS = 16
DIM = 128
TILE = 128
COLS = 8
ROWS = 16
FRAMES = 2
GROUP = FRAMES * COLS
EXTRA = 16
SECOND = 2 * TILE + EXTRA
BIG = 1e30
SCALE = DIM**-0.5
C = SCALE * 1.4426950408889634

F32 = jnp.float32
BF16 = jnp.bfloat16
VMEM_LIMIT = 20 * 1024 * 1024


def params(**kw):
    return pltpu.CompilerParams(vmem_limit_bytes=VMEM_LIMIT, **kw)


def small():
    return pltpu.CompilerParams(vmem_limit_bytes=8 * 1024 * 1024)


SMEM = pl.BlockSpec(memory_space=pltpu.SMEM)
VM = pl.BlockSpec(memory_space=pltpu.VMEM)
ANY = pl.BlockSpec(memory_space=pl.ANY)


CHUNKS = 4


def pack_first_kernel(k_ref, v_ref, out_ref, buf_ref, in_sem, out_sem):
    wide = HEADS // CHUNKS * DIM
    refs = (k_ref, v_ref)

    def fetch(part, i):
        cols = pl.ds(i * wide, wide)
        return pltpu.make_async_copy(refs[part].at[:, cols], buf_ref.at[part, :, cols], in_sem.at[part, i])

    def send(part, h):
        return pltpu.make_async_copy(
            buf_ref.at[part, :, pl.ds(h * DIM, DIM)], out_ref.at[h, pl.ds(part * TILE, TILE), :], out_sem.at[part, h]
        )

    for i in range(CHUNKS):
        for part in range(2):
            fetch(part, i).start()
    for i in range(CHUNKS):
        for part in range(2):
            fetch(part, i).wait()
            for h in range(i * HEADS // CHUNKS, (i + 1) * HEADS // CHUNKS):
                send(part, h).start()
    for h in range(HEADS):
        for part in range(2):
            send(part, h).wait()


def pack_first(keys, values):
    return pl.pallas_call(
        pack_first_kernel,
        in_specs=[ANY, ANY],
        out_specs=ANY,
        out_shape=jax.ShapeDtypeStruct((HEADS, 2 * TILE, DIM), BF16),
        scratch_shapes=[
            pltpu.VMEM((2, TILE, HEADS * DIM), BF16),
            pltpu.SemaphoreType.DMA((2, CHUNKS)),
            pltpu.SemaphoreType.DMA((2, HEADS)),
        ],
        compiler_params=pltpu.CompilerParams(vmem_limit_bytes=58 * 1024 * 1024),
        cost_estimate=pl.CostEstimate(flops=0, bytes_accessed=2**21, transcendentals=0),
        name="pack_keys_values",
    )(keys, values)


def pack_second_kernel(w_ref, q_ref, g_ref, o_ref, m_ref, out_ref):
    mine = m_ref[pl.ds(w_ref[0], 1), :].astype(F32)
    rows = lax.broadcasted_iota(jnp.int32, (EXTRA, TILE), 0)
    for h in range(out_ref.shape[0]):
        cols = slice(h * DIM, (h + 1) * DIM)
        g = g_ref[:, cols]
        out_ref[h, :TILE, :] = q_ref[:, cols]
        out_ref[h, TILE : 2 * TILE, :] = g
        prod = g.astype(F32) * o_ref[:, cols].astype(F32)
        delta = jnp.sum(prod.T, axis=0, keepdims=True)
        high = delta.astype(BF16).astype(F32)
        extra = jnp.where(rows == 0, high, 0.0)
        extra = jnp.where(rows == 1, delta - high, extra)
        extra = jnp.where(rows == 2, mine[:, :TILE], extra)
        out_ref[h, 2 * TILE :, :] = jnp.where(rows == 3, mine[:, TILE:], extra).astype(BF16)


def pack_second(w, q, g, o, mask):
    step = 4
    block = pl.BlockSpec((TILE, step * DIM), lambda i: (0, i))
    return pl.pallas_call(
        pack_second_kernel,
        grid=(HEADS // step,),
        in_specs=[SMEM, block, block, block, pl.BlockSpec((COLS, 2 * TILE), lambda i: (0, 0))],
        out_specs=pl.BlockSpec((step, SECOND, DIM), lambda i: (i, 0, 0)),
        out_shape=jax.ShapeDtypeStruct((HEADS, SECOND, DIM), BF16),
        compiler_params=small(),
        cost_estimate=pl.CostEstimate(flops=2**20, bytes_accessed=5 * 2**19, transcendentals=0),
        name="pack_queries",
    )(w, q, g, o, mask)


def unpack_kernel(in_ref, q_ref, k_ref, v_ref, sem):
    refs = (q_ref, k_ref, v_ref)

    def move(part, h):
        return pltpu.make_async_copy(
            in_ref.at[h, pl.ds(part * TILE, TILE), :], refs[part].at[:, pl.ds(h * DIM, DIM)], sem.at[part, h]
        )

    for h in range(HEADS):
        for part in range(3):
            move(part, h).start()
    for h in range(HEADS):
        for part in range(3):
            move(part, h).wait()


def unpack(x):
    out = jax.ShapeDtypeStruct((TILE, HEADS * DIM), BF16)
    return pl.pallas_call(
        unpack_kernel,
        in_specs=[VM],
        out_specs=[ANY] * 3,
        out_shape=[out] * 3,
        scratch_shapes=[pltpu.SemaphoreType.DMA((3, HEADS))],
        compiler_params=small(),
        cost_estimate=pl.CostEstimate(flops=0, bytes_accessed=3 * 2**20, transcendentals=0),
        name="unpack_grads",
    )(x)


def add_kernel(mine_ref, near_ref, far_ref, out_ref):
    out_ref[:, :TILE, :] = mine_ref[:, :TILE, :]
    total = mine_ref[:, TILE:, :].astype(F32) + near_ref[...].astype(F32) + far_ref[...].astype(F32)
    out_ref[:, TILE:, :] = total.astype(BF16)


def add_parts(mine, near, far):
    step = 4
    block = pl.BlockSpec((step, 2 * TILE, DIM), lambda i: (i, 0, 0))
    wide = pl.BlockSpec((step, 3 * TILE, DIM), lambda i: (i, 0, 0))
    return pl.pallas_call(
        add_kernel,
        grid=(GROUP // step,),
        in_specs=[wide, block, block],
        out_specs=wide,
        out_shape=jax.ShapeDtypeStruct((GROUP, 3 * TILE, DIM), BF16),
        compiler_params=small(),
        cost_estimate=pl.CostEstimate(flops=2**20, bytes_accessed=5 * 2**20, transcendentals=0),
        name="add_parts",
    )(mine, near, far)


def dot_nt(a, b):
    return lax.dot_general(a, b, (((1,), (1,)), ((), ())), preferred_element_type=F32)


def dot_nn(a, b):
    return lax.dot_general(a, b, (((1,), (0,)), ((), ())), preferred_element_type=F32)


EDGE_LEFT = ((1, 0, True, False), (2, 1, True, False))
EDGE_RIGHT = ((0, COLS - 2, False, True), (1, COLS - 1, False, True))


def inner_steps(w):
    return ((0, w - 1, False, True), (1, w, False, False), (2, w + 1, True, False))


def sweep(body):
    body(0, EDGE_LEFT)

    def inner(w, carry):
        body(w, inner_steps(w))
        return carry

    lax.fori_loop(1, COLS - 1, inner, 0)
    body(COLS - 1, EDGE_RIGHT)


def both(ref, col, part):
    rows = slice(part * TILE, (part + 1) * TILE)
    return jnp.concatenate([ref[col, rows, :], ref[COLS + col, rows, :]], axis=0)


def penalties(rows_ref, m_ref, unit, w, col):
    found = []
    inside = rows_ref[unit + 3] != 0
    for key_frame in range(FRAMES):
        at = key_frame * TILE + rows_ref[unit] * COLS + col
        cells = []
        for frame in range(FRAMES):
            live = (m_ref[frame * COLS + w, at] != 0) & inside
            cells.append(jnp.broadcast_to(jnp.where(live, 0.0, BIG).astype(F32), (1, TILE)))
        found.append(jnp.concatenate(cells, axis=1))
    return found


def fold(x, op):
    return op(x.reshape(TILE // 8, 8, 2 * TILE), axis=0)


def query_side(qd_ref, w):
    q = both(qd_ref, w, 0)
    g = both(qd_ref, w, 1)
    delta = []
    for frame in range(FRAMES):
        extra = qd_ref[frame * COLS + w, 2 * TILE :, :].astype(F32)
        delta.append(extra[0:1, :] + extra[1:2, :])
    return q, g, jnp.concatenate(delta, axis=1)


def step_grads(kv_ref, kt_ref, dk_ref, dv_ref, out_ref, at, prob, q, g, delta, col, first, last):
    dprob = dot_nt(both(kv_ref, col, 1), g)
    dscore = (prob * (dprob - delta)).astype(BF16)
    prob = prob.astype(BF16)
    dv = dot_nn(prob, g)
    dk = dot_nn(dscore, q)
    if first:
        turned_keys = jnp.concatenate([kv_ref[col, :TILE, :].T, kv_ref[COLS + col, :TILE, :].T], axis=1)
        kt_ref[col] = turned_keys
    else:
        turned_keys = kt_ref[col]
    for frame in range(FRAMES):
        rows = slice(frame * TILE, (frame + 1) * TILE)
        tile = frame * COLS + col
        dv_here, dk_here = dv[rows], dk[rows]
        if not first:
            dv_here += dv_ref[tile]
            dk_here += dk_ref[tile]
        if last:
            out_ref[tile, at * TILE : (at + 1) * TILE, :] = (dk_here * SCALE).astype(BF16)
            out_ref[tile, (at + 1) * TILE : (at + 2) * TILE, :] = dv_here.astype(BF16)
        else:
            dv_ref[tile] = dv_here
            dk_ref[tile] = dk_here
    return dot_nn(turned_keys, dscore)


def halves(x):
    return [x[:TILE], x[TILE:]]


def early_kernel(rows_ref, m_ref, qd_ref, own_ref, near_ref, e_ref, peak_ref, total_ref, s_ref):
    units = ((0, near_ref), (1, own_ref))

    def body(w, steps):
        q = both(qd_ref, w, 0)
        top = jnp.full((8, 2 * TILE), -BIG, F32)
        pens = {}
        for unit, kv_ref in units:
            for place, col, _, _ in steps:
                s = dot_nt(both(kv_ref, col, 0), q)
                s_ref[unit, place] = s
                pens[unit, place] = penalties(rows_ref, m_ref, unit, w, col)
                for piece, pen in zip(halves(s), pens[unit, place]):
                    top = jnp.maximum(top, fold(piece, jnp.max) - pen)
        peak = jnp.max(top, axis=0, keepdims=True)
        total = jnp.zeros((8, 2 * TILE), F32)
        for unit, _ in units:
            for place, _, _, _ in steps:
                for frame in range(FRAMES):
                    rows = slice(frame * TILE, (frame + 1) * TILE)
                    e = jnp.exp2(s_ref[unit, place, rows, :] * C - (peak * C + pens[unit, place][frame]))
                    e_ref[w, unit, place, rows, :] = e.astype(BF16)
                    total += fold(e, jnp.sum)
        peak_ref[w] = jnp.broadcast_to(peak, (8, 2 * TILE))
        total_ref[w] = jnp.broadcast_to(jnp.sum(total, axis=0, keepdims=True), (8, 2 * TILE))

    sweep(body)


def far_kernel(
    rows_ref, m_ref, qd_ref, far_ref, peak_ref, total_ref, part_ref, share_ref, dqt_ref,
    even_ref, odd_ref, kt_ref, dk_ref, dv_ref,
):
    def weigh(w, s_ref):
        q = both(qd_ref, w, 0)
        early = peak_ref[w]
        top = early
        pens = []
        for place in range(3):
            wanted = w + place - 1
            col = jnp.clip(wanted, 0, COLS - 1)
            s = dot_nt(both(far_ref, col, 0), q)
            s_ref[place] = s
            outside = jnp.where(wanted == col, 0.0, BIG).astype(F32)
            pens.append([pen + outside for pen in penalties(rows_ref, m_ref, 2, w, col)])
            for piece, pen in zip(halves(s), pens[place]):
                top = jnp.maximum(top, fold(piece, jnp.max) - pen)
        peak = jnp.max(top, axis=0, keepdims=True)
        total = jnp.zeros((8, 2 * TILE), F32)
        for place in range(3):
            for frame in range(FRAMES):
                rows = slice(frame * TILE, (frame + 1) * TILE)
                e = jnp.exp2(s_ref[place, rows, :] * C - (peak * C + pens[place][frame]))
                s_ref[place, rows, :] = e
                total += fold(e, jnp.sum)
        shrink = jnp.exp2((early[0:1, :] - peak) * C)
        share = 1.0 / (jnp.sum(total, axis=0, keepdims=True) + total_ref[w, 0:1, :] * shrink)
        share_ref[w] = jnp.broadcast_to(shrink * share, (8, 2 * TILE))
        return share

    def grads(w, share, s_ref, steps):
        q, g, delta = query_side(qd_ref, w)
        dqt = jnp.zeros((DIM, 2 * TILE), F32)
        for place, col, first, last in steps:
            prob = s_ref[place] * share
            dqt += step_grads(far_ref, kt_ref, dk_ref, dv_ref, part_ref, 0, prob, q, g, delta, col, first, last)
        dqt_ref[w] = dqt

    edge = COLS - 1
    share = weigh(0, even_ref)
    later = weigh(1, odd_ref)
    grads(0, share, even_ref, EDGE_LEFT)

    def two(i, share):
        w = 2 * i + 1
        later = weigh(w + 1, even_ref)
        grads(w, share, odd_ref, inner_steps(w))
        share = weigh(w + 2, odd_ref)
        grads(w + 1, later, even_ref, inner_steps(w + 1))
        return share

    share = lax.fori_loop(0, (COLS - 2) // 2, two, later)
    grads(edge, share, odd_ref, EDGE_RIGHT)


def rest_kernel(
    qd_ref, own_ref, near_ref, e_ref, share_ref, dqt_ref, part_ref, mine_ref,
    ktc_ref, kto_ref, dkc_ref, dvc_ref, dko_ref, dvo_ref,
):
    def body(w, steps):
        q, g, delta = query_side(qd_ref, w)
        share = share_ref[w, 0:1, :]
        dqt = dqt_ref[w]
        for place, col, first, last in steps:
            prob = e_ref[w, 0, place].astype(F32) * share
            dqt += step_grads(near_ref, ktc_ref, dkc_ref, dvc_ref, part_ref, 0, prob, q, g, delta, col, first, last)
            prob = e_ref[w, 1, place].astype(F32) * share
            dqt += step_grads(own_ref, kto_ref, dko_ref, dvo_ref, mine_ref, 1, prob, q, g, delta, col, first, last)
        dq = (dqt.T * SCALE).astype(BF16)
        mine_ref[w, :TILE, :] = dq[:TILE]
        mine_ref[COLS + w, :TILE, :] = dq[TILE:]

    sweep(body)


def acc():
    return pltpu.VMEM((GROUP, TILE, DIM), F32)


def turned():
    return pltpu.VMEM((COLS, DIM, 2 * TILE), BF16)


ROWS_OF = jax.ShapeDtypeStruct((COLS, 8, 2 * TILE), F32)
PART = jax.ShapeDtypeStruct((GROUP, 2 * TILE, DIM), BF16)


def early(rows, live, qd, own, near):
    return pl.pallas_call(
        early_kernel,
        in_specs=[SMEM, SMEM, VM, VM, VM],
        out_specs=[VM, VM, VM],
        out_shape=[jax.ShapeDtypeStruct((COLS, 2, 3, 2 * TILE, 2 * TILE), BF16), ROWS_OF, ROWS_OF],
        scratch_shapes=[pltpu.VMEM((2, 3, 2 * TILE, 2 * TILE), F32)],
        compiler_params=params(),
        cost_estimate=pl.CostEstimate(flops=2 * 10**9, bytes_accessed=3 * 2**20, transcendentals=3 * 10**6),
        name="near_and_own_scores",
    )(rows, live, qd, own, near)


def far_row(rows, live, qd, far, peak, total):
    return pl.pallas_call(
        far_kernel,
        in_specs=[SMEM, SMEM, VM, VM, VM, VM],
        out_specs=[VM, VM, VM],
        out_shape=[PART, ROWS_OF, jax.ShapeDtypeStruct((COLS, DIM, 2 * TILE), F32)],
        scratch_shapes=[pltpu.VMEM((3, 2 * TILE, 2 * TILE), F32)] * 2 + [turned(), acc(), acc()],
        compiler_params=params(),
        cost_estimate=pl.CostEstimate(flops=2 * 10**9, bytes_accessed=2**22, transcendentals=2 * 10**6),
        name="far_row",
    )(rows, live, qd, far, peak, total)


def rest(qd, own, near, e, share, dqt):
    return pl.pallas_call(
        rest_kernel,
        in_specs=[VM] * 6,
        out_specs=[VM, VM],
        out_shape=[PART, jax.ShapeDtypeStruct((GROUP, 3 * TILE, DIM), BF16)],
        scratch_shapes=[turned(), turned(), acc(), acc(), acc(), acc()],
        compiler_params=params(),
        cost_estimate=pl.CostEstimate(flops=4 * 10**9, bytes_accessed=2**23, transcendentals=0),
        name="near_and_own_rows",
    )(qd, own, near, e, share, dqt)


def per_device(queries, keys, values, d_out, saved_out, mask):
    group = ("frame", "head")
    row = lax.axis_index("row")
    is_even = lax.rem(row, 2) == 0
    chip_swap = [(i, i ^ 1) for i in range(ROWS)]
    link_swap = [(i, i + 1) for i in range(1, ROWS - 1, 2)] + [(i + 1, i) for i in range(1, ROWS - 1, 2)]

    def exchange(x):
        return lax.all_to_all(x, group, split_axis=0, concat_axis=0, tiled=True)

    w = lax.axis_index("head").astype(jnp.int32).reshape(1)
    own = exchange(pack_first(keys, values))
    second = pack_second(w, queries, d_out, saved_out, mask)
    own, second = lax.optimization_barrier((own, second))
    qd = exchange(second)
    far = lax.ppermute(own, "row", link_swap)
    near = lax.ppermute(own, "row", chip_swap)

    far_index = jnp.where(is_even, row - 1, row + 1)
    near_index = jnp.where(is_even, row + 1, row - 1)
    rows = jnp.stack([near_index, row, far_index]).astype(jnp.int32)
    inside = ((rows >= 0) & (rows < ROWS)).astype(jnp.int32)
    rows = jnp.concatenate([jnp.clip(rows, 0, ROWS - 1), inside])
    live = qd[:, 2 * TILE + 2 : 2 * TILE + 4, :].astype(jnp.int32).reshape(GROUP, 2 * TILE)

    e, peak, total = early(rows, live, qd, own, near)
    far_part, share, dqt = far_row(rows, live, qd, far, peak, total)
    far_back = lax.ppermute(far_part, "row", link_swap)
    near_part, mine = rest(qd, own, near, e, share, dqt)
    far_back, mine = lax.optimization_barrier((far_back, mine))
    near_back = lax.ppermute(near_part, "row", chip_swap)
    return tuple(unpack(exchange(add_parts(mine, near_back, far_back))))


def solution(mesh):
    devices = mesh.devices
    if mesh.axis_names != ("head", "blk"):
        raise ValueError("mesh axes")
    heads = devices.shape[0]
    grid = Mesh(devices.reshape(heads, FRAMES, devices.shape[1] // FRAMES), ("head", "frame", "row"))
    tokens = P(("frame", "row", "head"), None)
    return jax.shard_map(
        per_device,
        mesh=grid,
        in_specs=(tokens,) * 5 + (P(("frame", "row"), None),),
        out_specs=(tokens,) * 3,
        check_vma=False,
    )
```

```python
import functools

import jax
import jax.numpy as jnp
from jax import lax
from jax.experimental import pallas as pl
from jax.experimental.pallas import tpu as pltpu
from jax.sharding import Mesh, PartitionSpec as P

HEADS = 16
DIM = 128
TILE = 128
COLS = 8
ROWS = 16
FRAMES = 2
GROUP = FRAMES * COLS
EXTRA = 16
NEAR_FLOPS = 2 * 10**9
OWN_FLOPS = 2 * 10**9
SECOND = 2 * TILE + EXTRA
BIG = 1e30
SCALE = DIM**-0.5
C = SCALE * 1.4426950408889634

F32 = jnp.float32
BF16 = jnp.bfloat16
VMEM_LIMIT = 20 * 1024 * 1024


def params(**kw):
    return pltpu.CompilerParams(vmem_limit_bytes=VMEM_LIMIT, **kw)


def small():
    return pltpu.CompilerParams(vmem_limit_bytes=8 * 1024 * 1024)


SMEM = pl.BlockSpec(memory_space=pltpu.SMEM)
VM = pl.BlockSpec(memory_space=pltpu.VMEM)
ANY = pl.BlockSpec(memory_space=pl.ANY)


CHUNKS = 4


def pack_first_kernel(k_ref, v_ref, out_ref, buf_ref, in_sem, out_sem):
    wide = HEADS // CHUNKS * DIM
    refs = (k_ref, v_ref)

    def fetch(part, i):
        cols = pl.ds(i * wide, wide)
        return pltpu.make_async_copy(refs[part].at[:, cols], buf_ref.at[part, :, cols], in_sem.at[part, i])

    def send(part, h):
        return pltpu.make_async_copy(
            buf_ref.at[part, :, pl.ds(h * DIM, DIM)], out_ref.at[h, pl.ds(part * TILE, TILE), :], out_sem.at[part, h]
        )

    for i in range(CHUNKS):
        for part in range(2):
            fetch(part, i).start()
    for i in range(CHUNKS):
        for part in range(2):
            fetch(part, i).wait()
            for h in range(i * HEADS // CHUNKS, (i + 1) * HEADS // CHUNKS):
                send(part, h).start()
    for h in range(HEADS):
        for part in range(2):
            send(part, h).wait()


def pack_first(keys, values):
    return pl.pallas_call(
        pack_first_kernel,
        in_specs=[ANY, ANY],
        out_specs=ANY,
        out_shape=jax.ShapeDtypeStruct((HEADS, 2 * TILE, DIM), BF16),
        scratch_shapes=[
            pltpu.VMEM((2, TILE, HEADS * DIM), BF16),
            pltpu.SemaphoreType.DMA((2, CHUNKS)),
            pltpu.SemaphoreType.DMA((2, HEADS)),
        ],
        compiler_params=pltpu.CompilerParams(vmem_limit_bytes=58 * 1024 * 1024),
        cost_estimate=pl.CostEstimate(flops=0, bytes_accessed=2**21, transcendentals=0),
        name="pack_keys_values",
    )(keys, values)


def pack_second_kernel(w_ref, q_ref, g_ref, o_ref, m_ref, out_ref):
    mine = m_ref[pl.ds(w_ref[0], 1), :].astype(F32)
    rows = lax.broadcasted_iota(jnp.int32, (EXTRA, TILE), 0)
    for h in range(out_ref.shape[0]):
        cols = slice(h * DIM, (h + 1) * DIM)
        g = g_ref[:, cols]
        out_ref[h, :TILE, :] = q_ref[:, cols]
        out_ref[h, TILE : 2 * TILE, :] = g
        prod = g.astype(F32) * o_ref[:, cols].astype(F32)
        delta = jnp.sum(prod.T, axis=0, keepdims=True)
        high = delta.astype(BF16).astype(F32)
        extra = jnp.where(rows == 0, high, 0.0)
        extra = jnp.where(rows == 1, delta - high, extra)
        extra = jnp.where(rows == 2, mine[:, :TILE], extra)
        out_ref[h, 2 * TILE :, :] = jnp.where(rows == 3, mine[:, TILE:], extra).astype(BF16)


def pack_second(w, q, g, o, mask):
    step = 4
    block = pl.BlockSpec((TILE, step * DIM), lambda i: (0, i))
    return pl.pallas_call(
        pack_second_kernel,
        grid=(HEADS // step,),
        in_specs=[SMEM, block, block, block, pl.BlockSpec((COLS, 2 * TILE), lambda i: (0, 0))],
        out_specs=pl.BlockSpec((step, SECOND, DIM), lambda i: (i, 0, 0)),
        out_shape=jax.ShapeDtypeStruct((HEADS, SECOND, DIM), BF16),
        compiler_params=small(),
        cost_estimate=pl.CostEstimate(flops=2**20, bytes_accessed=5 * 2**19, transcendentals=0),
        name="pack_queries",
    )(w, q, g, o, mask)


def unpack_kernel(in_ref, q_ref, k_ref, v_ref, sem):
    refs = (q_ref, k_ref, v_ref)

    def move(part, h):
        return pltpu.make_async_copy(
            in_ref.at[h, pl.ds(part * TILE, TILE), :], refs[part].at[:, pl.ds(h * DIM, DIM)], sem.at[part, h]
        )

    for h in range(HEADS):
        for part in range(3):
            move(part, h).start()
    for h in range(HEADS):
        for part in range(3):
            move(part, h).wait()


def unpack(x):
    out = jax.ShapeDtypeStruct((TILE, HEADS * DIM), BF16)
    return pl.pallas_call(
        unpack_kernel,
        in_specs=[VM],
        out_specs=[ANY] * 3,
        out_shape=[out] * 3,
        scratch_shapes=[pltpu.SemaphoreType.DMA((3, HEADS))],
        compiler_params=small(),
        cost_estimate=pl.CostEstimate(flops=0, bytes_accessed=3 * 2**20, transcendentals=0),
        name="unpack_grads",
    )(x)


def add_kernel(mine_ref, near_ref, far_ref, out_ref):
    out_ref[:, :TILE, :] = mine_ref[:, :TILE, :]
    for i in range(out_ref.shape[0]):
        far = far_ref[i * 2 * TILE : (i + 1) * 2 * TILE, :].astype(F32)
        total = mine_ref[i, TILE:, :].astype(F32) + near_ref[i].astype(F32) + far
        out_ref[i, TILE:, :] = total.astype(BF16)


def add_parts(mine, near, far):
    step = 4
    block = pl.BlockSpec((step, 2 * TILE, DIM), lambda i: (i, 0, 0))
    wide = pl.BlockSpec((step, 3 * TILE, DIM), lambda i: (i, 0, 0))
    return pl.pallas_call(
        add_kernel,
        grid=(GROUP // step,),
        in_specs=[wide, block, pl.BlockSpec((step * 2 * TILE, DIM), lambda i: (i, 0))],
        out_specs=wide,
        out_shape=jax.ShapeDtypeStruct((GROUP, 3 * TILE, DIM), BF16),
        compiler_params=small(),
        cost_estimate=pl.CostEstimate(flops=2**20, bytes_accessed=5 * 2**20, transcendentals=0),
        name="add_parts",
    )(mine, near, far)


def dot_nt(a, b):
    return lax.dot_general(a, b, (((1,), (1,)), ((), ())), preferred_element_type=F32)


def dot_nn(a, b):
    return lax.dot_general(a, b, (((1,), (0,)), ((), ())), preferred_element_type=F32)


EDGE_LEFT = ((1, 0, True, False), (2, 1, True, False))
EDGE_RIGHT = ((0, COLS - 2, False, True), (1, COLS - 1, False, True))


def inner_steps(w):
    return ((0, w - 1, False, True), (1, w, False, False), (2, w + 1, True, False))


def sweep(body):
    body(0, EDGE_LEFT)

    def inner(w, carry):
        body(w, inner_steps(w))
        return carry

    lax.fori_loop(1, COLS - 1, inner, 0)
    body(COLS - 1, EDGE_RIGHT)


def both(ref, col, part):
    rows = slice(part * TILE, (part + 1) * TILE)
    return jnp.concatenate([ref[col, rows, :], ref[COLS + col, rows, :]], axis=0)


def penalties(rows_ref, m_ref, unit, w, place):
    wanted = w + place - 1
    col = jnp.clip(wanted, 0, COLS - 1)
    inside = (rows_ref[unit + 3] != 0) & (wanted == col)
    found = []
    for key_frame in range(FRAMES):
        at = key_frame * TILE + rows_ref[unit] * COLS + col
        found.append(
            [
                jnp.where((m_ref[frame * COLS + w, at] != 0) & inside, 0.0, BIG).astype(F32)
                for frame in range(FRAMES)
            ]
        )
    return found


def shifted(x, pens, sign):
    return jnp.concatenate([x[:, :TILE] + sign * pens[0], x[:, TILE:] + sign * pens[1]], axis=1)


def exponentials(piece, level):
    e = jnp.exp2(piece.reshape(TILE // 8, 8, 2 * TILE) * C - level[None])
    return e.reshape(TILE, 2 * TILE), jnp.sum(e, axis=0)


def score(rows_ref, m_ref, unit, kv_ref, q, w, s_ref, top):
    cols = [jnp.clip(w + place - 1, 0, COLS - 1) for place in range(3)]
    scores = dot_nt(jnp.concatenate([both(kv_ref, col, 0) for col in cols], axis=0), q)
    for place in range(3):
        pens = penalties(rows_ref, m_ref, unit, w, place)
        for frame in range(FRAMES):
            piece = scores[(FRAMES * place + frame) * TILE : (FRAMES * place + frame + 1) * TILE]
            s_ref[place, frame * TILE : (frame + 1) * TILE, :] = piece
            top = jnp.maximum(top, shifted(fold(piece, jnp.max), pens[frame], -1.0))
    return top


def spread(x):
    return jnp.broadcast_to(x, (8, 2 * TILE))


def fold(x, op):
    return op(x.reshape(TILE // 8, 8, 2 * TILE), axis=0)


def query_side(qd_ref, w):
    q = both(qd_ref, w, 0)
    g = both(qd_ref, w, 1)
    delta = []
    for frame in range(FRAMES):
        extra = qd_ref[frame * COLS + w, 2 * TILE :, :].astype(F32)
        delta.append(extra[0:1, :] + extra[1:2, :])
    return q, g, jnp.concatenate(delta, axis=1)


def column_grads(kv_ref, kt_ref, dk_ref, dv_ref, out_ref, at, prob, q, g, delta, steps):
    dprob = dot_nt(jnp.concatenate([both(kv_ref, col, 1) for _, col, _, _ in steps], axis=0), g)
    dscore = (prob * (dprob - delta)).astype(BF16)
    dv = dot_nn(prob.astype(BF16), g)
    dk = dot_nn(dscore, q)
    turned_keys = []
    for i, (_, col, first, last) in enumerate(steps):
        if first:
            kt_ref[col] = jnp.concatenate([kv_ref[col, :TILE, :].T, kv_ref[COLS + col, :TILE, :].T], axis=1)
        turned_keys.append(kt_ref[col])
        for frame in range(FRAMES):
            rows = slice((FRAMES * i + frame) * TILE, (FRAMES * i + frame + 1) * TILE)
            tile = frame * COLS + col
            dv_here, dk_here = dv[rows], dk[rows]
            if not first:
                dv_here += dv_ref[tile]
                dk_here += dk_ref[tile]
            if last and at is None:
                out_ref[pl.ds(tile * 2 * TILE, TILE), :] = (dk_here * SCALE).astype(BF16)
                out_ref[pl.ds(tile * 2 * TILE + TILE, TILE), :] = dv_here.astype(BF16)
            elif last:
                out_ref[tile, at * TILE : (at + 1) * TILE, :] = (dk_here * SCALE).astype(BF16)
                out_ref[tile, (at + 1) * TILE : (at + 2) * TILE, :] = dv_here.astype(BF16)
            else:
                dv_ref[tile] = dv_here
                dk_ref[tile] = dk_here
    return dot_nn(jnp.concatenate(turned_keys, axis=1), dscore)


def early_kernel(rows_ref, m_ref, qd_ref, own_ref, near_ref, e_ref, peak_ref, total_ref, even_ref, odd_ref):
    def scores(w, s_ref):
        q = both(qd_ref, w, 0)
        top = jnp.full((8, 2 * TILE), -BIG, F32)
        for unit, kv_ref in enumerate((near_ref, own_ref)):
            top = score(rows_ref, m_ref, unit, kv_ref, q, w, s_ref.at[unit], top)
        peak_ref[w] = spread(jnp.max(top, axis=0, keepdims=True))

    def weigh(w, s_ref):
        level = peak_ref[w] * C
        total = jnp.zeros((8, 2 * TILE), F32)
        for unit in range(2):
            for place in range(3):
                pens = penalties(rows_ref, m_ref, unit, w, place)
                for frame in range(FRAMES):
                    rows = slice(frame * TILE, (frame + 1) * TILE)
                    e, part = exponentials(s_ref[unit, place, rows, :], shifted(level, pens[frame], 1.0))
                    e_ref[w, unit, place, rows, :] = e.astype(BF16)
                    total += part
        total_ref[w] = spread(jnp.sum(total, axis=0, keepdims=True))

    def two(i, carry):
        w = 2 * i
        scores(w + 1, odd_ref)
        weigh(w, even_ref)
        scores(jnp.minimum(w + 2, COLS - 1), even_ref)
        weigh(w + 1, odd_ref)
        return carry

    scores(0, even_ref)
    lax.fori_loop(0, COLS // 2, two, 0)


def far_kernel(
    rows_ref, m_ref, qd_ref, far_ref, peak_ref, total_ref, part_ref, share_ref, dqt_ref,
    even_ref, odd_ref, kt_ref, dk_ref, dv_ref,
):
    part_ref[GROUP * 2 * TILE :, :] = jnp.zeros((EXTRA, DIM), BF16)

    def weigh(w, s_ref):
        early = peak_ref[w]
        top = score(rows_ref, m_ref, 2, far_ref, both(qd_ref, w, 0), w, s_ref, early)
        peak = spread(jnp.max(top, axis=0, keepdims=True))
        total = jnp.zeros((8, 2 * TILE), F32)
        for place in range(3):
            pens = penalties(rows_ref, m_ref, 2, w, place)
            for frame in range(FRAMES):
                rows = slice(frame * TILE, (frame + 1) * TILE)
                e, part = exponentials(s_ref[place, rows, :], shifted(peak * C, pens[frame], 1.0))
                s_ref[place, rows, :] = e
                total += part
        shrink = jnp.exp2((early - peak) * C)
        share = 1.0 / (jnp.sum(total, axis=0, keepdims=True) + total_ref[w] * shrink)
        share_ref[w] = shrink * share
        return share[0:1, :]

    def grads(w, share, s_ref, steps):
        q, g, delta = query_side(qd_ref, w)
        prob = jnp.concatenate([s_ref[place] for place, _, _, _ in steps], axis=0) * share
        dqt_ref[w] = column_grads(far_ref, kt_ref, dk_ref, dv_ref, part_ref, None, prob, q, g, delta, steps)

    edge = COLS - 1
    share = weigh(0, even_ref)
    later = weigh(1, odd_ref)
    grads(0, share, even_ref, EDGE_LEFT)

    def two(i, share):
        w = 2 * i + 1
        later = weigh(w + 1, even_ref)
        grads(w, share, odd_ref, inner_steps(w))
        share = weigh(w + 2, odd_ref)
        grads(w + 1, later, even_ref, inner_steps(w + 1))
        return share

    share = lax.fori_loop(0, (COLS - 2) // 2, two, later)
    grads(edge, share, odd_ref, EDGE_RIGHT)


def row_kernel(unit, qd_ref, kv_ref, e_ref, share_ref, dqt_ref, out_ref, sum_ref, kt_ref, dk_ref, dv_ref):
    def body(w, steps):
        q, g, delta = query_side(qd_ref, w)
        share = share_ref[w, 0:1, :]
        prob = jnp.concatenate([e_ref[w, unit, place] for place, _, _, _ in steps], axis=0).astype(F32) * share
        dqt = dqt_ref[w] + column_grads(kv_ref, kt_ref, dk_ref, dv_ref, out_ref, unit, prob, q, g, delta, steps)
        if unit == 1:
            dq = (dqt.T * SCALE).astype(BF16)
            out_ref[w, :TILE, :] = dq[:TILE]
            out_ref[COLS + w, :TILE, :] = dq[TILE:]
        else:
            sum_ref[w] = dqt

    sweep(body)


def near_kernel(qd_ref, kv_ref, e_ref, share_ref, dqt_ref, out_ref, sum_ref, kt_ref, dk_ref, dv_ref):
    row_kernel(0, qd_ref, kv_ref, e_ref, share_ref, dqt_ref, out_ref, sum_ref, kt_ref, dk_ref, dv_ref)


def own_kernel(qd_ref, kv_ref, e_ref, share_ref, dqt_ref, out_ref, kt_ref, dk_ref, dv_ref):
    row_kernel(1, qd_ref, kv_ref, e_ref, share_ref, dqt_ref, out_ref, None, kt_ref, dk_ref, dv_ref)


def acc():
    return pltpu.VMEM((GROUP, TILE, DIM), F32)


def turned():
    return pltpu.VMEM((COLS, DIM, 2 * TILE), BF16)


ROWS_OF = jax.ShapeDtypeStruct((COLS, 8, 2 * TILE), F32)
PART = jax.ShapeDtypeStruct((GROUP, 2 * TILE, DIM), BF16)
FAR_PART = jax.ShapeDtypeStruct((GROUP * 2 * TILE + EXTRA, DIM), BF16)


def early(rows, live, qd, own, near):
    return pl.pallas_call(
        early_kernel,
        in_specs=[SMEM, SMEM, VM, VM, VM],
        out_specs=[VM, VM, VM],
        out_shape=[jax.ShapeDtypeStruct((COLS, 2, 3, 2 * TILE, 2 * TILE), BF16), ROWS_OF, ROWS_OF],
        scratch_shapes=[pltpu.VMEM((2, 3, 2 * TILE, 2 * TILE), F32)] * 2,
        compiler_params=params(),
        cost_estimate=pl.CostEstimate(flops=2 * 10**9, bytes_accessed=3 * 2**20, transcendentals=3 * 10**6),
        name="near_and_own_scores",
    )(rows, live, qd, own, near)


def far_row(rows, live, qd, far, peak, total):
    return pl.pallas_call(
        far_kernel,
        in_specs=[SMEM, SMEM, VM, VM, VM, VM],
        out_specs=[VM, VM, VM],
        out_shape=[FAR_PART, ROWS_OF, jax.ShapeDtypeStruct((COLS, DIM, 2 * TILE), F32)],
        scratch_shapes=[pltpu.VMEM((3, 2 * TILE, 2 * TILE), F32)] * 2 + [turned(), acc(), acc()],
        compiler_params=params(),
        cost_estimate=pl.CostEstimate(flops=2 * 10**9, bytes_accessed=2**22, transcendentals=2 * 10**6),
        name="far_row",
    )(rows, live, qd, far, peak, total)


SUMS = jax.ShapeDtypeStruct((COLS, DIM, 2 * TILE), F32)


def near_row(qd, near, e, share, dqt):
    return pl.pallas_call(
        near_kernel,
        in_specs=[VM] * 5,
        out_specs=[VM, VM],
        out_shape=[PART, SUMS],
        scratch_shapes=[turned(), acc(), acc()],
        compiler_params=params(),
        cost_estimate=pl.CostEstimate(flops=NEAR_FLOPS, bytes_accessed=2**22, transcendentals=0),
        name="near_row",
    )(qd, near, e, share, dqt)


def own_row(qd, own, e, share, dqt):
    return pl.pallas_call(
        own_kernel,
        in_specs=[VM] * 5,
        out_specs=VM,
        out_shape=jax.ShapeDtypeStruct((GROUP, 3 * TILE, DIM), BF16),
        scratch_shapes=[turned(), acc(), acc()],
        compiler_params=params(),
        cost_estimate=pl.CostEstimate(flops=OWN_FLOPS, bytes_accessed=2**22, transcendentals=0),
        name="own_row",
    )(qd, own, e, share, dqt)


def per_device(queries, keys, values, d_out, saved_out, mask):
    group = ("frame", "head")
    row = lax.axis_index("row")
    is_even = lax.rem(row, 2) == 0
    chip_swap = [(i, i ^ 1) for i in range(ROWS)]
    link_swap = [(i, i + 1) for i in range(1, ROWS - 1, 2)] + [(i + 1, i) for i in range(1, ROWS - 1, 2)]

    def exchange(x):
        return lax.all_to_all(x, group, split_axis=0, concat_axis=0, tiled=True)

    w = lax.axis_index("head").astype(jnp.int32).reshape(1)
    own = exchange(pack_first(keys, values))
    second = pack_second(w, queries, d_out, saved_out, mask)
    own, second = lax.optimization_barrier((own, second))
    qd = exchange(second)
    far = lax.ppermute(own, "row", link_swap)
    near = lax.ppermute(own, "row", chip_swap)

    far_index = jnp.where(is_even, row - 1, row + 1)
    near_index = jnp.where(is_even, row + 1, row - 1)
    rows = jnp.stack([near_index, row, far_index]).astype(jnp.int32)
    inside = ((rows >= 0) & (rows < ROWS)).astype(jnp.int32)
    rows = jnp.concatenate([jnp.clip(rows, 0, ROWS - 1), inside])
    live = qd[:, 2 * TILE + 2 : 2 * TILE + 4, :].astype(jnp.int32).reshape(GROUP, 2 * TILE)

    e, peak, total = early(rows, live, qd, own, near)
    far_part, share, dqt = far_row(rows, live, qd, far, peak, total)
    far_back = lax.ppermute(far_part, "row", link_swap)
    near_part, dqt = near_row(qd, near, e, share, dqt)
    near_back = lax.ppermute(near_part, "row", chip_swap)
    mine = own_row(qd, own, e, share, dqt)
    return tuple(unpack(exchange(add_parts(mine, near_back, far_back))))


def solution(mesh):
    devices = mesh.devices
    if mesh.axis_names != ("head", "blk"):
        raise ValueError("mesh axes")
    heads = devices.shape[0]
    grid = Mesh(devices.reshape(heads, FRAMES, devices.shape[1] // FRAMES), ("head", "frame", "row"))
    tokens = P(("frame", "row", "head"), None)
    return jax.shard_map(
        per_device,
        mesh=grid,
        in_specs=(tokens,) * 5 + (P(("frame", "row"), None),),
        out_specs=(tokens,) * 3,
        check_vma=False,
    )
```

```python
import functools

import jax
import jax.numpy as jnp
from jax import lax
from jax.experimental import pallas as pl
from jax.experimental.pallas import tpu as pltpu
from jax.sharding import Mesh, PartitionSpec as P

HEADS = 16
DIM = 128
TILE = 128
COLS = 8
ROWS = 16
FRAMES = 2
GROUP = FRAMES * COLS
EXTRA = 8
NEAR_FLOPS = 2 * 10**9
OWN_FLOPS = 2 * 10**9
SECOND = 2 * TILE + EXTRA
BIG = 1e30
SCALE = DIM**-0.5
C = SCALE * 1.4426950408889634

F32 = jnp.float32
BF16 = jnp.bfloat16
VMEM_LIMIT = 20 * 1024 * 1024


def params(**kw):
    return pltpu.CompilerParams(vmem_limit_bytes=VMEM_LIMIT, **kw)


def small():
    return pltpu.CompilerParams(vmem_limit_bytes=8 * 1024 * 1024)


SMEM = pl.BlockSpec(memory_space=pltpu.SMEM)
VM = pl.BlockSpec(memory_space=pltpu.VMEM)
ANY = pl.BlockSpec(memory_space=pl.ANY)


CHUNKS = 4


def pack_first_kernel(k_ref, v_ref, out_ref, flat_ref, packed_ref, in_sem, out_sem):
    rows_in = TILE // CHUNKS
    refs = (k_ref, v_ref)

    def fetch(part, i):
        rows = pl.ds(i * rows_in, rows_in)
        return pltpu.make_async_copy(refs[part].at[rows, :], flat_ref.at[part, rows, :], in_sem.at[part, i])

    def send(part, i):
        rows = pl.ds(part * TILE + i * rows_in, rows_in)
        return pltpu.make_async_copy(packed_ref.at[:, rows, :], out_ref.at[:, rows, :], out_sem.at[part, i])

    for i in range(CHUNKS):
        for part in range(2):
            fetch(part, i).start()
    for i in range(CHUNKS):
        for part in range(2):
            fetch(part, i).wait()
            for h in range(HEADS):
                packed_ref[h, part * TILE + i * rows_in : part * TILE + (i + 1) * rows_in, :] = flat_ref[
                    part, i * rows_in : (i + 1) * rows_in, h * DIM : (h + 1) * DIM
                ]
            send(part, i).start()
    for i in range(CHUNKS):
        for part in range(2):
            send(part, i).wait()


def pack_first(keys, values):
    return pl.pallas_call(
        pack_first_kernel,
        in_specs=[ANY, ANY],
        out_specs=ANY,
        out_shape=jax.ShapeDtypeStruct((HEADS, 2 * TILE, DIM), BF16),
        scratch_shapes=[
            pltpu.VMEM((2, TILE, HEADS * DIM), BF16),
            pltpu.VMEM((HEADS, 2 * TILE, DIM), BF16),
            pltpu.SemaphoreType.DMA((2, CHUNKS)),
            pltpu.SemaphoreType.DMA((2, CHUNKS)),
        ],
        compiler_params=pltpu.CompilerParams(vmem_limit_bytes=58 * 1024 * 1024),
        cost_estimate=pl.CostEstimate(flops=0, bytes_accessed=2**21, transcendentals=0),
        name="pack_keys_values",
    )(keys, values)


def pack_second_kernel(w_ref, q_ref, g_ref, o_ref, m_ref, out_ref):
    mine = m_ref[pl.ds(w_ref[0], 1), :].astype(F32)
    rows = lax.broadcasted_iota(jnp.int32, (EXTRA, TILE), 0)
    for h in range(out_ref.shape[0]):
        cols = slice(h * DIM, (h + 1) * DIM)
        g = g_ref[:, cols]
        out_ref[h, :TILE, :] = q_ref[:, cols]
        out_ref[h, TILE : 2 * TILE, :] = g
        prod = g.astype(F32) * o_ref[:, cols].astype(F32)
        delta = jnp.sum(prod.T, axis=0, keepdims=True)
        high = delta.astype(BF16).astype(F32)
        extra = jnp.where(rows == 0, high, 0.0)
        extra = jnp.where(rows == 1, delta - high, extra)
        extra = jnp.where(rows == 2, mine[:, :TILE], extra)
        out_ref[h, 2 * TILE :, :] = jnp.where(rows == 3, mine[:, TILE:], extra).astype(BF16)


def pack_second(w, q, g, o, mask):
    step = 4
    block = pl.BlockSpec((TILE, step * DIM), lambda i: (0, i))
    return pl.pallas_call(
        pack_second_kernel,
        grid=(HEADS // step,),
        in_specs=[SMEM, block, block, block, pl.BlockSpec((COLS, 2 * TILE), lambda i: (0, 0))],
        out_specs=pl.BlockSpec((step, SECOND, DIM), lambda i: (i, 0, 0)),
        out_shape=jax.ShapeDtypeStruct((HEADS, SECOND, DIM), BF16),
        compiler_params=small(),
        cost_estimate=pl.CostEstimate(flops=2**20, bytes_accessed=5 * 2**19, transcendentals=0),
        name="pack_queries",
    )(w, q, g, o, mask)


def unpack_kernel(in_ref, q_ref, k_ref, v_ref, flat_ref, sem):
    rows_out = TILE // CHUNKS
    refs = (q_ref, k_ref, v_ref)

    def send(part, i):
        rows = pl.ds(i * rows_out, rows_out)
        return pltpu.make_async_copy(flat_ref.at[part, rows, :], refs[part].at[rows, :], sem.at[part, i])

    for part in range(3):
        for i in range(CHUNKS):
            for h in range(HEADS):
                flat_ref[part, i * rows_out : (i + 1) * rows_out, h * DIM : (h + 1) * DIM] = in_ref[
                    h, part * TILE + i * rows_out : part * TILE + (i + 1) * rows_out, :
                ]
            send(part, i).start()
    for part in range(3):
        for i in range(CHUNKS):
            send(part, i).wait()


def unpack(x):
    out = jax.ShapeDtypeStruct((TILE, HEADS * DIM), BF16)
    return pl.pallas_call(
        unpack_kernel,
        in_specs=[VM],
        out_specs=[ANY] * 3,
        out_shape=[out] * 3,
        scratch_shapes=[pltpu.VMEM((3, TILE, HEADS * DIM), BF16), pltpu.SemaphoreType.DMA((3, CHUNKS))],
        compiler_params=small(),
        cost_estimate=pl.CostEstimate(flops=0, bytes_accessed=3 * 2**20, transcendentals=0),
        name="unpack_grads",
    )(x)


def add_kernel(mine_ref, near_ref, far_ref, out_ref):
    out_ref[:, :TILE, :] = mine_ref[:, :TILE, :]
    for i in range(out_ref.shape[0]):
        far = far_ref[i * 2 * TILE : (i + 1) * 2 * TILE, :].astype(F32)
        total = mine_ref[i, TILE:, :].astype(F32) + near_ref[i].astype(F32) + far
        out_ref[i, TILE:, :] = total.astype(BF16)


def add_parts(mine, near, far):
    step = 4
    block = pl.BlockSpec((step, 2 * TILE, DIM), lambda i: (i, 0, 0))
    wide = pl.BlockSpec((step, 3 * TILE, DIM), lambda i: (i, 0, 0))
    return pl.pallas_call(
        add_kernel,
        grid=(GROUP // step,),
        in_specs=[wide, block, pl.BlockSpec((step * 2 * TILE, DIM), lambda i: (i, 0))],
        out_specs=wide,
        out_shape=jax.ShapeDtypeStruct((GROUP, 3 * TILE, DIM), BF16),
        compiler_params=small(),
        cost_estimate=pl.CostEstimate(flops=2**20, bytes_accessed=5 * 2**20, transcendentals=0),
        name="add_parts",
    )(mine, near, far)


def dot_nt(a, b):
    return lax.dot_general(a, b, (((1,), (1,)), ((), ())), preferred_element_type=F32)


def dot_nn(a, b):
    return lax.dot_general(a, b, (((1,), (0,)), ((), ())), preferred_element_type=F32)


EDGE_LEFT = ((1, 0, True, False), (2, 1, True, False))
EDGE_RIGHT = ((0, COLS - 2, False, True), (1, COLS - 1, False, True))


def inner_steps(w):
    return ((0, w - 1, False, True), (1, w, False, False), (2, w + 1, True, False))


def sweep(body):
    body(0, EDGE_LEFT)

    def inner(w, carry):
        body(w, inner_steps(w))
        return carry

    lax.fori_loop(1, COLS - 1, inner, 0)
    body(COLS - 1, EDGE_RIGHT)


def both(ref, col, part):
    rows = slice(part * TILE, (part + 1) * TILE)
    return jnp.concatenate([ref[col, rows, :], ref[COLS + col, rows, :]], axis=0)


def penalties(rows_ref, m_ref, unit, w, place):
    wanted = w + place - 1
    col = jnp.clip(wanted, 0, COLS - 1)
    inside = (rows_ref[unit + 3] != 0) & (wanted == col)
    found = []
    for key_frame in range(FRAMES):
        at = key_frame * TILE + rows_ref[unit] * COLS + col
        found.append(
            [
                jnp.where((m_ref[frame * COLS + w, at] != 0) & inside, 0.0, BIG).astype(F32)
                for frame in range(FRAMES)
            ]
        )
    return found


def shifted(x, pens, sign):
    return jnp.concatenate([x[:, :TILE] + sign * pens[0], x[:, TILE:] + sign * pens[1]], axis=1)


def exponentials(piece, level):
    e = jnp.exp2(piece.reshape(TILE // 8, 8, 2 * TILE) * C - level[None])
    return e.reshape(TILE, 2 * TILE), jnp.sum(e, axis=0)


def score(rows_ref, m_ref, unit, kv_ref, q, w, s_ref, top):
    cols = [jnp.clip(w + place - 1, 0, COLS - 1) for place in range(3)]
    scores = dot_nt(jnp.concatenate([both(kv_ref, col, 0) for col in cols], axis=0), q)
    for place in range(3):
        pens = penalties(rows_ref, m_ref, unit, w, place)
        for frame in range(FRAMES):
            piece = scores[(FRAMES * place + frame) * TILE : (FRAMES * place + frame + 1) * TILE]
            s_ref[place, frame * TILE : (frame + 1) * TILE, :] = piece
            top = jnp.maximum(top, shifted(fold(piece, jnp.max), pens[frame], -1.0))
    return top


def spread(x):
    return jnp.broadcast_to(x, (8, 2 * TILE))


def fold(x, op):
    return op(x.reshape(TILE // 8, 8, 2 * TILE), axis=0)


def query_side(qd_ref, w):
    q = both(qd_ref, w, 0)
    g = both(qd_ref, w, 1)
    delta = []
    for frame in range(FRAMES):
        extra = qd_ref[frame * COLS + w, 2 * TILE :, :].astype(F32)
        delta.append(extra[0:1, :] + extra[1:2, :])
    return q, g, jnp.concatenate(delta, axis=1)


def column_grads(kv_ref, kt_ref, dk_ref, dv_ref, out_ref, at, prob, q, g, delta, steps):
    dprob = dot_nt(jnp.concatenate([both(kv_ref, col, 1) for _, col, _, _ in steps], axis=0), g)
    dscore = (prob * (dprob - delta)).astype(BF16)
    dv = dot_nn(prob.astype(BF16), g)
    dk = dot_nn(dscore, q)
    turned_keys = []
    for i, (_, col, first, last) in enumerate(steps):
        if first:
            kt_ref[col] = jnp.concatenate([kv_ref[col, :TILE, :].T, kv_ref[COLS + col, :TILE, :].T], axis=1)
        turned_keys.append(kt_ref[col])
        for frame in range(FRAMES):
            rows = slice((FRAMES * i + frame) * TILE, (FRAMES * i + frame + 1) * TILE)
            tile = frame * COLS + col
            dv_here, dk_here = dv[rows], dk[rows]
            if not first:
                dv_here += dv_ref[tile]
                dk_here += dk_ref[tile]
            if last and at is None:
                out_ref[pl.ds(tile * 2 * TILE, TILE), :] = (dk_here * SCALE).astype(BF16)
                out_ref[pl.ds(tile * 2 * TILE + TILE, TILE), :] = dv_here.astype(BF16)
            elif last:
                out_ref[tile, at * TILE : (at + 1) * TILE, :] = (dk_here * SCALE).astype(BF16)
                out_ref[tile, (at + 1) * TILE : (at + 2) * TILE, :] = dv_here.astype(BF16)
            else:
                dv_ref[tile] = dv_here
                dk_ref[tile] = dk_here
    return dot_nn(jnp.concatenate(turned_keys, axis=1), dscore)


def early_kernel(rows_ref, m_ref, qd_ref, own_ref, near_ref, e_ref, peak_ref, total_ref, even_ref, odd_ref):
    def scores(w, s_ref):
        q = both(qd_ref, w, 0)
        top = jnp.full((8, 2 * TILE), -BIG, F32)
        for unit, kv_ref in enumerate((near_ref, own_ref)):
            top = score(rows_ref, m_ref, unit, kv_ref, q, w, s_ref.at[unit], top)
        peak_ref[w] = spread(jnp.max(top, axis=0, keepdims=True))

    def weigh(w, s_ref):
        level = peak_ref[w] * C
        total = jnp.zeros((8, 2 * TILE), F32)
        for unit in range(2):
            for place in range(3):
                pens = penalties(rows_ref, m_ref, unit, w, place)
                for frame in range(FRAMES):
                    rows = slice(frame * TILE, (frame + 1) * TILE)
                    e, part = exponentials(s_ref[unit, place, rows, :], shifted(level, pens[frame], 1.0))
                    e_ref[w, unit, place, rows, :] = e.astype(BF16)
                    total += part
        total_ref[w] = spread(jnp.sum(total, axis=0, keepdims=True))

    def two(i, carry):
        w = 2 * i
        scores(w + 1, odd_ref)
        weigh(w, even_ref)
        scores(jnp.minimum(w + 2, COLS - 1), even_ref)
        weigh(w + 1, odd_ref)
        return carry

    scores(0, even_ref)
    lax.fori_loop(0, COLS // 2, two, 0)


def far_kernel(
    rows_ref, m_ref, qd_ref, far_ref, peak_ref, total_ref, part_ref, share_ref, dqt_ref,
    even_ref, odd_ref, kt_ref, dk_ref, dv_ref,
):
    part_ref[GROUP * 2 * TILE :, :] = jnp.zeros((EXTRA, DIM), BF16)

    def weigh(w, s_ref):
        early = peak_ref[w]
        top = score(rows_ref, m_ref, 2, far_ref, both(qd_ref, w, 0), w, s_ref, early)
        peak = spread(jnp.max(top, axis=0, keepdims=True))
        total = jnp.zeros((8, 2 * TILE), F32)
        for place in range(3):
            pens = penalties(rows_ref, m_ref, 2, w, place)
            for frame in range(FRAMES):
                rows = slice(frame * TILE, (frame + 1) * TILE)
                e, part = exponentials(s_ref[place, rows, :], shifted(peak * C, pens[frame], 1.0))
                s_ref[place, rows, :] = e
                total += part
        shrink = jnp.exp2((early - peak) * C)
        share = 1.0 / (jnp.sum(total, axis=0, keepdims=True) + total_ref[w] * shrink)
        share_ref[w] = shrink * share
        return share[0:1, :]

    def grads(w, share, s_ref, steps):
        q, g, delta = query_side(qd_ref, w)
        prob = jnp.concatenate([s_ref[place] for place, _, _, _ in steps], axis=0) * share
        dqt_ref[w] = column_grads(far_ref, kt_ref, dk_ref, dv_ref, part_ref, None, prob, q, g, delta, steps)

    edge = COLS - 1
    share = weigh(0, even_ref)
    later = weigh(1, odd_ref)
    grads(0, share, even_ref, EDGE_LEFT)

    def two(i, share):
        w = 2 * i + 1
        later = weigh(w + 1, even_ref)
        grads(w, share, odd_ref, inner_steps(w))
        share = weigh(w + 2, odd_ref)
        grads(w + 1, later, even_ref, inner_steps(w + 1))
        return share

    share = lax.fori_loop(0, (COLS - 2) // 2, two, later)
    grads(edge, share, odd_ref, EDGE_RIGHT)


def row_kernel(unit, qd_ref, kv_ref, e_ref, share_ref, dqt_ref, out_ref, sum_ref, kt_ref, dk_ref, dv_ref):
    def body(w, steps):
        q, g, delta = query_side(qd_ref, w)
        share = share_ref[w, 0:1, :]
        prob = jnp.concatenate([e_ref[w, unit, place] for place, _, _, _ in steps], axis=0).astype(F32) * share
        dqt = dqt_ref[w] + column_grads(kv_ref, kt_ref, dk_ref, dv_ref, out_ref, unit, prob, q, g, delta, steps)
        if unit == 1:
            dq = (dqt.T * SCALE).astype(BF16)
            out_ref[w, :TILE, :] = dq[:TILE]
            out_ref[COLS + w, :TILE, :] = dq[TILE:]
        else:
            sum_ref[w] = dqt

    sweep(body)


def near_kernel(qd_ref, kv_ref, e_ref, share_ref, dqt_ref, out_ref, sum_ref, kt_ref, dk_ref, dv_ref):
    row_kernel(0, qd_ref, kv_ref, e_ref, share_ref, dqt_ref, out_ref, sum_ref, kt_ref, dk_ref, dv_ref)


def own_kernel(qd_ref, kv_ref, e_ref, share_ref, dqt_ref, out_ref, kt_ref, dk_ref, dv_ref):
    row_kernel(1, qd_ref, kv_ref, e_ref, share_ref, dqt_ref, out_ref, None, kt_ref, dk_ref, dv_ref)


def acc():
    return pltpu.VMEM((GROUP, TILE, DIM), F32)


def turned():
    return pltpu.VMEM((COLS, DIM, 2 * TILE), BF16)


ROWS_OF = jax.ShapeDtypeStruct((COLS, 8, 2 * TILE), F32)
PART = jax.ShapeDtypeStruct((GROUP, 2 * TILE, DIM), BF16)
FAR_PART = jax.ShapeDtypeStruct((GROUP * 2 * TILE + EXTRA, DIM), BF16)


def early(rows, live, qd, own, near):
    return pl.pallas_call(
        early_kernel,
        in_specs=[SMEM, SMEM, VM, VM, VM],
        out_specs=[VM, VM, VM],
        out_shape=[jax.ShapeDtypeStruct((COLS, 2, 3, 2 * TILE, 2 * TILE), BF16), ROWS_OF, ROWS_OF],
        scratch_shapes=[pltpu.VMEM((2, 3, 2 * TILE, 2 * TILE), F32)] * 2,
        compiler_params=params(),
        cost_estimate=pl.CostEstimate(flops=2 * 10**9, bytes_accessed=3 * 2**20, transcendentals=3 * 10**6),
        name="near_and_own_scores",
    )(rows, live, qd, own, near)


def far_row(rows, live, qd, far, peak, total):
    return pl.pallas_call(
        far_kernel,
        in_specs=[SMEM, SMEM, VM, VM, VM, VM],
        out_specs=[VM, VM, VM],
        out_shape=[FAR_PART, ROWS_OF, jax.ShapeDtypeStruct((COLS, DIM, 2 * TILE), F32)],
        scratch_shapes=[pltpu.VMEM((3, 2 * TILE, 2 * TILE), F32)] * 2 + [turned(), acc(), acc()],
        compiler_params=params(),
        cost_estimate=pl.CostEstimate(flops=2 * 10**9, bytes_accessed=2**22, transcendentals=2 * 10**6),
        name="far_row",
    )(rows, live, qd, far, peak, total)


SUMS = jax.ShapeDtypeStruct((COLS, DIM, 2 * TILE), F32)


def near_row(qd, near, e, share, dqt):
    return pl.pallas_call(
        near_kernel,
        in_specs=[VM] * 5,
        out_specs=[VM, VM],
        out_shape=[PART, SUMS],
        scratch_shapes=[turned(), acc(), acc()],
        compiler_params=params(),
        cost_estimate=pl.CostEstimate(flops=NEAR_FLOPS, bytes_accessed=2**22, transcendentals=0),
        name="near_row",
    )(qd, near, e, share, dqt)


def own_row(qd, own, e, share, dqt):
    return pl.pallas_call(
        own_kernel,
        in_specs=[VM] * 5,
        out_specs=VM,
        out_shape=jax.ShapeDtypeStruct((GROUP, 3 * TILE, DIM), BF16),
        scratch_shapes=[turned(), acc(), acc()],
        compiler_params=params(),
        cost_estimate=pl.CostEstimate(flops=OWN_FLOPS, bytes_accessed=2**22, transcendentals=0),
        name="own_row",
    )(qd, own, e, share, dqt)


def per_device(queries, keys, values, d_out, saved_out, mask):
    group = ("frame", "head")
    row = lax.axis_index("row")
    is_even = lax.rem(row, 2) == 0
    chip_swap = [(i, i ^ 1) for i in range(ROWS)]
    link_swap = [(i, i + 1) for i in range(1, ROWS - 1, 2)] + [(i + 1, i) for i in range(1, ROWS - 1, 2)]

    def exchange(x):
        return lax.all_to_all(x, group, split_axis=0, concat_axis=0, tiled=True)

    w = lax.axis_index("head").astype(jnp.int32).reshape(1)
    own = exchange(pack_first(keys, values))
    second = pack_second(w, queries, d_out, saved_out, mask)
    own, second = lax.optimization_barrier((own, second))
    qd = exchange(second)
    far = lax.ppermute(own, "row", link_swap)
    near = lax.ppermute(own, "row", chip_swap)

    far_index = jnp.where(is_even, row - 1, row + 1)
    near_index = jnp.where(is_even, row + 1, row - 1)
    rows = jnp.stack([near_index, row, far_index]).astype(jnp.int32)
    inside = ((rows >= 0) & (rows < ROWS)).astype(jnp.int32)
    rows = jnp.concatenate([jnp.clip(rows, 0, ROWS - 1), inside])
    live = qd[:, 2 * TILE + 2 : 2 * TILE + 4, :].astype(jnp.int32).reshape(GROUP, 2 * TILE)

    e, peak, total = early(rows, live, qd, own, near)
    far_part, share, dqt = far_row(rows, live, qd, far, peak, total)
    far_back = lax.ppermute(far_part, "row", link_swap)
    near_part, dqt = near_row(qd, near, e, share, dqt)
    near_back = lax.ppermute(near_part, "row", chip_swap)
    mine = own_row(qd, own, e, share, dqt)
    return tuple(unpack(exchange(add_parts(mine, near_back, far_back))))


def solution(mesh):
    devices = mesh.devices
    if mesh.axis_names != ("head", "blk"):
        raise ValueError("mesh axes")
    heads = devices.shape[0]
    grid = Mesh(devices.reshape(heads, FRAMES, devices.shape[1] // FRAMES), ("head", "frame", "row"))
    tokens = P(("frame", "row", "head"), None)
    return jax.shard_map(
        per_device,
        mesh=grid,
        in_specs=(tokens,) * 5 + (P(("frame", "row"), None),),
        out_specs=(tokens,) * 3,
        check_vma=False,
    )
```

```python
import functools

import jax
import jax.numpy as jnp
from jax import lax
from jax.experimental import pallas as pl
from jax.experimental.pallas import tpu as pltpu
from jax.sharding import Mesh, PartitionSpec as P

HEADS = 16
DIM = 128
TILE = 128
COLS = 8
ROWS = 16
FRAMES = 2
GROUP = FRAMES * COLS
EXTRA = 8
NEAR_FLOPS = 2 * 10**9
OWN_FLOPS = 2 * 10**9
SECOND = 2 * TILE + EXTRA
BIG = 1e30
SCALE = DIM**-0.5
C = SCALE * 1.4426950408889634

F32 = jnp.float32
BF16 = jnp.bfloat16
VMEM_LIMIT = 20 * 1024 * 1024


def params(**kw):
    return pltpu.CompilerParams(vmem_limit_bytes=VMEM_LIMIT, **kw)


def small():
    return pltpu.CompilerParams(vmem_limit_bytes=8 * 1024 * 1024)


SMEM = pl.BlockSpec(memory_space=pltpu.SMEM)
VM = pl.BlockSpec(memory_space=pltpu.VMEM)
ANY = pl.BlockSpec(memory_space=pl.ANY)


CHUNKS = 4


def pack_first_kernel(k_ref, v_ref, out_ref, flat_ref, packed_ref, in_sem, out_sem):
    rows_in = TILE // CHUNKS
    refs = (k_ref, v_ref)

    def fetch(part, i):
        rows = pl.ds(i * rows_in, rows_in)
        return pltpu.make_async_copy(refs[part].at[rows, :], flat_ref.at[part, rows, :], in_sem.at[part, i])

    def send(part, i):
        rows = pl.ds(part * TILE + i * rows_in, rows_in)
        return pltpu.make_async_copy(packed_ref.at[:, rows, :], out_ref.at[:, rows, :], out_sem.at[part, i])

    for i in range(CHUNKS):
        for part in range(2):
            fetch(part, i).start()
    for i in range(CHUNKS):
        for part in range(2):
            fetch(part, i).wait()
            for h in range(HEADS):
                packed_ref[h, part * TILE + i * rows_in : part * TILE + (i + 1) * rows_in, :] = flat_ref[
                    part, i * rows_in : (i + 1) * rows_in, h * DIM : (h + 1) * DIM
                ]
            send(part, i).start()
    for i in range(CHUNKS):
        for part in range(2):
            send(part, i).wait()


def pack_first(keys, values):
    return pl.pallas_call(
        pack_first_kernel,
        in_specs=[ANY, ANY],
        out_specs=ANY,
        out_shape=jax.ShapeDtypeStruct((HEADS, 2 * TILE, DIM), BF16),
        scratch_shapes=[
            pltpu.VMEM((2, TILE, HEADS * DIM), BF16),
            pltpu.VMEM((HEADS, 2 * TILE, DIM), BF16),
            pltpu.SemaphoreType.DMA((2, CHUNKS)),
            pltpu.SemaphoreType.DMA((2, CHUNKS)),
        ],
        compiler_params=pltpu.CompilerParams(vmem_limit_bytes=58 * 1024 * 1024),
        cost_estimate=pl.CostEstimate(flops=0, bytes_accessed=2**21, transcendentals=0),
        name="pack_keys_values",
    )(keys, values)


def pack_second_kernel(w_ref, q_ref, g_ref, o_ref, m_ref, out_ref):
    mine = m_ref[pl.ds(w_ref[0], 1), :].astype(F32)
    rows = lax.broadcasted_iota(jnp.int32, (EXTRA, TILE), 0)
    for h in range(out_ref.shape[0]):
        cols = slice(h * DIM, (h + 1) * DIM)
        g = g_ref[:, cols]
        out_ref[h, :TILE, :] = q_ref[:, cols]
        out_ref[h, TILE : 2 * TILE, :] = g
        prod = g.astype(F32) * o_ref[:, cols].astype(F32)
        delta = jnp.sum(prod.T, axis=0, keepdims=True)
        high = delta.astype(BF16).astype(F32)
        extra = jnp.where(rows == 0, high, 0.0)
        extra = jnp.where(rows == 1, delta - high, extra)
        extra = jnp.where(rows == 2, mine[:, :TILE], extra)
        out_ref[h, 2 * TILE :, :] = jnp.where(rows == 3, mine[:, TILE:], extra).astype(BF16)


def pack_second(w, q, g, o, mask):
    step = 4
    block = pl.BlockSpec((TILE, step * DIM), lambda i: (0, i))
    return pl.pallas_call(
        pack_second_kernel,
        grid=(HEADS // step,),
        in_specs=[SMEM, block, block, block, pl.BlockSpec((COLS, 2 * TILE), lambda i: (0, 0))],
        out_specs=pl.BlockSpec((step, SECOND, DIM), lambda i: (i, 0, 0)),
        out_shape=jax.ShapeDtypeStruct((HEADS, SECOND, DIM), BF16),
        compiler_params=small(),
        cost_estimate=pl.CostEstimate(flops=2**20, bytes_accessed=5 * 2**19, transcendentals=0),
        name="pack_queries",
    )(w, q, g, o, mask)


def unpack_kernel(in_ref, q_ref, k_ref, v_ref, flat_ref, sem):
    rows_out = TILE // CHUNKS
    refs = (q_ref, k_ref, v_ref)

    def send(part, i):
        rows = pl.ds(i * rows_out, rows_out)
        return pltpu.make_async_copy(flat_ref.at[part, rows, :], refs[part].at[rows, :], sem.at[part, i])

    for part in range(3):
        for i in range(CHUNKS):
            for h in range(HEADS):
                flat_ref[part, i * rows_out : (i + 1) * rows_out, h * DIM : (h + 1) * DIM] = in_ref[
                    h, part * TILE + i * rows_out : part * TILE + (i + 1) * rows_out, :
                ]
            send(part, i).start()
    for part in range(3):
        for i in range(CHUNKS):
            send(part, i).wait()


def unpack(x):
    out = jax.ShapeDtypeStruct((TILE, HEADS * DIM), BF16)
    return pl.pallas_call(
        unpack_kernel,
        in_specs=[VM],
        out_specs=[ANY] * 3,
        out_shape=[out] * 3,
        scratch_shapes=[pltpu.VMEM((3, TILE, HEADS * DIM), BF16), pltpu.SemaphoreType.DMA((3, CHUNKS))],
        compiler_params=small(),
        cost_estimate=pl.CostEstimate(flops=0, bytes_accessed=3 * 2**20, transcendentals=0),
        name="unpack_grads",
    )(x)


def add_kernel(mine_ref, near_ref, far_ref, out_ref):
    out_ref[:, :TILE, :] = mine_ref[:, :TILE, :]
    for i in range(out_ref.shape[0]):
        far = far_ref[i * 2 * TILE : (i + 1) * 2 * TILE, :].astype(F32)
        total = mine_ref[i, TILE:, :].astype(F32) + near_ref[i].astype(F32) + far
        out_ref[i, TILE:, :] = total.astype(BF16)


def add_parts(mine, near, far):
    step = 4
    block = pl.BlockSpec((step, 2 * TILE, DIM), lambda i: (i, 0, 0))
    wide = pl.BlockSpec((step, 3 * TILE, DIM), lambda i: (i, 0, 0))
    return pl.pallas_call(
        add_kernel,
        grid=(GROUP // step,),
        in_specs=[wide, block, pl.BlockSpec((step * 2 * TILE, DIM), lambda i: (i, 0))],
        out_specs=wide,
        out_shape=jax.ShapeDtypeStruct((GROUP, 3 * TILE, DIM), BF16),
        compiler_params=small(),
        cost_estimate=pl.CostEstimate(flops=2**20, bytes_accessed=5 * 2**20, transcendentals=0),
        name="add_parts",
    )(mine, near, far)


def dot_nt(a, b):
    return lax.dot_general(a, b, (((1,), (1,)), ((), ())), preferred_element_type=F32)


def dot_nn(a, b):
    return lax.dot_general(a, b, (((1,), (0,)), ((), ())), preferred_element_type=F32)


EDGE_LEFT = ((1, 0, True, False), (2, 1, True, False))
EDGE_RIGHT = ((0, COLS - 2, False, True), (1, COLS - 1, False, True))


def inner_steps(w):
    return ((0, w - 1, False, True), (1, w, False, False), (2, w + 1, True, False))


def sweep(body):
    body(0, EDGE_LEFT)

    def inner(w, carry):
        body(w, inner_steps(w))
        return carry

    lax.fori_loop(1, COLS - 1, inner, 0)
    body(COLS - 1, EDGE_RIGHT)


def both(ref, col, part):
    rows = slice(part * TILE, (part + 1) * TILE)
    return jnp.concatenate([ref[col, rows, :], ref[COLS + col, rows, :]], axis=0)


def penalties(rows_ref, m_ref, unit, w, place):
    wanted = w + place - 1
    col = jnp.clip(wanted, 0, COLS - 1)
    inside = (rows_ref[unit + 3] != 0) & (wanted == col)
    found = []
    for key_frame in range(FRAMES):
        at = key_frame * TILE + rows_ref[unit] * COLS + col
        found.append(
            [
                jnp.where((m_ref[frame * COLS + w, at] != 0) & inside, 0.0, BIG).astype(F32)
                for frame in range(FRAMES)
            ]
        )
    return found


def shifted(x, pens, sign):
    return jnp.concatenate([x[:, :TILE] + sign * pens[0], x[:, TILE:] + sign * pens[1]], axis=1)


def exponentials(piece, level):
    e = jnp.exp2(piece.reshape(TILE // 8, 8, 2 * TILE) * C - level[None])
    return e.reshape(TILE, 2 * TILE), jnp.sum(e, axis=0)


def score(rows_ref, m_ref, unit, kv_ref, q, w, s_ref, top, wide):
    cols = [jnp.clip(w + place - 1, 0, COLS - 1) for place in range(3)]
    keys = [both(kv_ref, col, 0) for col in cols]
    if wide:
        scores = dot_nt(jnp.concatenate(keys, axis=0), q)
        scores = [scores[2 * TILE * place : 2 * TILE * (place + 1)] for place in range(3)]
    else:
        scores = [dot_nt(key, q) for key in keys]
    for place in range(3):
        pens = penalties(rows_ref, m_ref, unit, w, place)
        for frame in range(FRAMES):
            piece = scores[place][frame * TILE : (frame + 1) * TILE]
            s_ref[place, frame * TILE : (frame + 1) * TILE, :] = piece
            top = jnp.maximum(top, shifted(fold(piece, jnp.max), pens[frame], -1.0))
    return top


def spread(x):
    return jnp.broadcast_to(x, (8, 2 * TILE))


def fold(x, op):
    return op(x.reshape(TILE // 8, 8, 2 * TILE), axis=0)


def query_side(qd_ref, w):
    q = both(qd_ref, w, 0)
    g = both(qd_ref, w, 1)
    delta = []
    for frame in range(FRAMES):
        extra = qd_ref[frame * COLS + w, 2 * TILE :, :].astype(F32)
        delta.append(extra[0:1, :] + extra[1:2, :])
    return q, g, jnp.concatenate(delta, axis=1)


def column_grads(kv_ref, kt_ref, dk_ref, dv_ref, out_ref, at, prob, q, g, delta, steps):
    dprob = dot_nt(jnp.concatenate([both(kv_ref, col, 1) for _, col, _, _ in steps], axis=0), g)
    dscore = (prob * (dprob - delta)).astype(BF16)
    dv = dot_nn(prob.astype(BF16), g)
    dk = dot_nn(dscore, q)
    turned_keys = []
    for i, (_, col, first, last) in enumerate(steps):
        if first:
            kt_ref[col] = jnp.concatenate([kv_ref[col, :TILE, :].T, kv_ref[COLS + col, :TILE, :].T], axis=1)
        turned_keys.append(kt_ref[col])
        for frame in range(FRAMES):
            rows = slice((FRAMES * i + frame) * TILE, (FRAMES * i + frame + 1) * TILE)
            tile = frame * COLS + col
            dv_here, dk_here = dv[rows], dk[rows]
            if not first:
                dv_here += dv_ref[tile]
                dk_here += dk_ref[tile]
            if last and at is None:
                out_ref[pl.ds(tile * 2 * TILE, TILE), :] = (dk_here * SCALE).astype(BF16)
                out_ref[pl.ds(tile * 2 * TILE + TILE, TILE), :] = dv_here.astype(BF16)
            elif last:
                out_ref[tile, at * TILE : (at + 1) * TILE, :] = (dk_here * SCALE).astype(BF16)
                out_ref[tile, (at + 1) * TILE : (at + 2) * TILE, :] = dv_here.astype(BF16)
            else:
                dv_ref[tile] = dv_here
                dk_ref[tile] = dk_here
    return dot_nn(jnp.concatenate(turned_keys, axis=1), dscore)


def early_kernel(rows_ref, m_ref, qd_ref, own_ref, near_ref, e_ref, peak_ref, total_ref, even_ref, odd_ref):
    def scores(w, s_ref):
        q = both(qd_ref, w, 0)
        top = jnp.full((8, 2 * TILE), -BIG, F32)
        for unit, kv_ref in enumerate((near_ref, own_ref)):
            top = score(rows_ref, m_ref, unit, kv_ref, q, w, s_ref.at[unit], top, True)
        peak_ref[w] = spread(jnp.max(top, axis=0, keepdims=True))

    def weigh(w, s_ref):
        level = peak_ref[w] * C
        total = jnp.zeros((8, 2 * TILE), F32)
        for unit in range(2):
            for place in range(3):
                pens = penalties(rows_ref, m_ref, unit, w, place)
                for frame in range(FRAMES):
                    below = shifted(level, pens[frame], 1.0)
                    for part in range(4):
                        rows = slice(frame * TILE + part * 32, frame * TILE + part * 32 + 32)
                        x = s_ref[unit, place, rows, :].reshape(4, 8, 2 * TILE)
                        e = jnp.exp2(x * C - below[None])
                        e_ref[w, unit, place, rows, :] = e.reshape(32, 2 * TILE).astype(BF16)
                        total += (e[0] + e[1]) + (e[2] + e[3])
        total_ref[w] = spread(jnp.sum(total, axis=0, keepdims=True))

    def two(i, carry):
        w = 2 * i
        scores(w + 1, odd_ref)
        weigh(w, even_ref)
        scores(jnp.minimum(w + 2, COLS - 1), even_ref)
        weigh(w + 1, odd_ref)
        return carry

    scores(0, even_ref)
    lax.fori_loop(0, COLS // 2, two, 0)


def far_kernel(
    rows_ref, m_ref, qd_ref, far_ref, peak_ref, total_ref, part_ref, share_ref, dqt_ref,
    even_ref, odd_ref, kt_ref, dk_ref, dv_ref,
):
    part_ref[GROUP * 2 * TILE :, :] = jnp.zeros((EXTRA, DIM), BF16)

    def weigh(w, s_ref):
        early = peak_ref[w]
        top = score(rows_ref, m_ref, 2, far_ref, both(qd_ref, w, 0), w, s_ref, early, False)
        peak = spread(jnp.max(top, axis=0, keepdims=True))
        total = jnp.zeros((8, 2 * TILE), F32)
        for place in range(3):
            pens = penalties(rows_ref, m_ref, 2, w, place)
            for frame in range(FRAMES):
                below = shifted(peak * C, pens[frame], 1.0)
                for part in range(4):
                    rows = slice(frame * TILE + part * 32, frame * TILE + part * 32 + 32)
                    x = s_ref[place, rows, :].reshape(4, 8, 2 * TILE)
                    e = jnp.exp2(x * C - below[None])
                    s_ref[place, rows, :] = e.reshape(32, 2 * TILE)
                    total += (e[0] + e[1]) + (e[2] + e[3])
        shrink = jnp.exp2((early - peak) * C)
        share = 1.0 / (jnp.sum(total, axis=0, keepdims=True) + total_ref[w] * shrink)
        share_ref[w] = shrink * share
        return share[0:1, :]

    def grads(w, share, s_ref, steps):
        q, g, delta = query_side(qd_ref, w)
        prob = jnp.concatenate([s_ref[place] for place, _, _, _ in steps], axis=0) * share
        dqt_ref[w] = column_grads(far_ref, kt_ref, dk_ref, dv_ref, part_ref, None, prob, q, g, delta, steps)

    edge = COLS - 1
    share = weigh(0, even_ref)
    later = weigh(1, odd_ref)
    grads(0, share, even_ref, EDGE_LEFT)

    def two(i, share):
        w = 2 * i + 1
        later = weigh(w + 1, even_ref)
        grads(w, share, odd_ref, inner_steps(w))
        share = weigh(w + 2, odd_ref)
        grads(w + 1, later, even_ref, inner_steps(w + 1))
        return share

    share = lax.fori_loop(0, (COLS - 2) // 2, two, later)
    grads(edge, share, odd_ref, EDGE_RIGHT)


def row_kernel(unit, qd_ref, kv_ref, e_ref, share_ref, dqt_ref, out_ref, sum_ref, kt_ref, dk_ref, dv_ref):
    def body(w, steps):
        q, g, delta = query_side(qd_ref, w)
        share = share_ref[w, 0:1, :]
        prob = jnp.concatenate([e_ref[w, unit, place] for place, _, _, _ in steps], axis=0).astype(F32) * share
        dqt = dqt_ref[w] + column_grads(kv_ref, kt_ref, dk_ref, dv_ref, out_ref, unit, prob, q, g, delta, steps)
        if unit == 1:
            dq = (dqt.T * SCALE).astype(BF16)
            out_ref[w, :TILE, :] = dq[:TILE]
            out_ref[COLS + w, :TILE, :] = dq[TILE:]
        else:
            sum_ref[w] = dqt

    sweep(body)


def near_kernel(qd_ref, kv_ref, e_ref, share_ref, dqt_ref, out_ref, sum_ref, kt_ref, dk_ref, dv_ref):
    row_kernel(0, qd_ref, kv_ref, e_ref, share_ref, dqt_ref, out_ref, sum_ref, kt_ref, dk_ref, dv_ref)


def own_kernel(qd_ref, kv_ref, e_ref, share_ref, dqt_ref, out_ref, kt_ref, dk_ref, dv_ref):
    row_kernel(1, qd_ref, kv_ref, e_ref, share_ref, dqt_ref, out_ref, None, kt_ref, dk_ref, dv_ref)


def acc():
    return pltpu.VMEM((GROUP, TILE, DIM), F32)


def turned():
    return pltpu.VMEM((COLS, DIM, 2 * TILE), BF16)


ROWS_OF = jax.ShapeDtypeStruct((COLS, 8, 2 * TILE), F32)
PART = jax.ShapeDtypeStruct((GROUP, 2 * TILE, DIM), BF16)
FAR_PART = jax.ShapeDtypeStruct((GROUP * 2 * TILE + EXTRA, DIM), BF16)


def early(rows, live, qd, own, near):
    return pl.pallas_call(
        early_kernel,
        in_specs=[SMEM, SMEM, VM, VM, VM],
        out_specs=[VM, VM, VM],
        out_shape=[jax.ShapeDtypeStruct((COLS, 2, 3, 2 * TILE, 2 * TILE), BF16), ROWS_OF, ROWS_OF],
        scratch_shapes=[pltpu.VMEM((2, 3, 2 * TILE, 2 * TILE), F32)] * 2,
        compiler_params=params(),
        cost_estimate=pl.CostEstimate(flops=2 * 10**9, bytes_accessed=3 * 2**20, transcendentals=3 * 10**6),
        name="near_and_own_scores",
    )(rows, live, qd, own, near)


def far_row(rows, live, qd, far, peak, total):
    return pl.pallas_call(
        far_kernel,
        in_specs=[SMEM, SMEM, VM, VM, VM, VM],
        out_specs=[VM, VM, VM],
        out_shape=[FAR_PART, ROWS_OF, jax.ShapeDtypeStruct((COLS, DIM, 2 * TILE), F32)],
        scratch_shapes=[pltpu.VMEM((3, 2 * TILE, 2 * TILE), F32)] * 2 + [turned(), acc(), acc()],
        compiler_params=params(),
        cost_estimate=pl.CostEstimate(flops=2 * 10**9, bytes_accessed=2**22, transcendentals=2 * 10**6),
        name="far_row",
    )(rows, live, qd, far, peak, total)


SUMS = jax.ShapeDtypeStruct((COLS, DIM, 2 * TILE), F32)


def near_row(qd, near, e, share, dqt):
    return pl.pallas_call(
        near_kernel,
        in_specs=[VM] * 5,
        out_specs=[VM, VM],
        out_shape=[PART, SUMS],
        scratch_shapes=[turned(), acc(), acc()],
        compiler_params=params(),
        cost_estimate=pl.CostEstimate(flops=NEAR_FLOPS, bytes_accessed=2**22, transcendentals=0),
        name="near_row",
    )(qd, near, e, share, dqt)


def own_row(qd, own, e, share, dqt):
    return pl.pallas_call(
        own_kernel,
        in_specs=[VM] * 5,
        out_specs=VM,
        out_shape=jax.ShapeDtypeStruct((GROUP, 3 * TILE, DIM), BF16),
        scratch_shapes=[turned(), acc(), acc()],
        compiler_params=params(),
        cost_estimate=pl.CostEstimate(flops=OWN_FLOPS, bytes_accessed=2**22, transcendentals=0),
        name="own_row",
    )(qd, own, e, share, dqt)


def per_device(queries, keys, values, d_out, saved_out, mask):
    group = ("frame", "head")
    row = lax.axis_index("row")
    is_even = lax.rem(row, 2) == 0
    chip_swap = [(i, i ^ 1) for i in range(ROWS)]
    link_swap = [(i, i + 1) for i in range(1, ROWS - 1, 2)] + [(i + 1, i) for i in range(1, ROWS - 1, 2)]

    def exchange(x):
        return lax.all_to_all(x, group, split_axis=0, concat_axis=0, tiled=True)

    w = lax.axis_index("head").astype(jnp.int32).reshape(1)
    own = exchange(pack_first(keys, values))
    second = pack_second(w, queries, d_out, saved_out, mask)
    own, second = lax.optimization_barrier((own, second))
    qd = exchange(second)
    far = lax.ppermute(own, "row", link_swap)
    near = lax.ppermute(own, "row", chip_swap)

    far_index = jnp.where(is_even, row - 1, row + 1)
    near_index = jnp.where(is_even, row + 1, row - 1)
    rows = jnp.stack([near_index, row, far_index]).astype(jnp.int32)
    inside = ((rows >= 0) & (rows < ROWS)).astype(jnp.int32)
    rows = jnp.concatenate([jnp.clip(rows, 0, ROWS - 1), inside])
    live = qd[:, 2 * TILE + 2 : 2 * TILE + 4, :].astype(jnp.int32).reshape(GROUP, 2 * TILE)

    e, peak, total = early(rows, live, qd, own, near)
    far_part, share, dqt = far_row(rows, live, qd, far, peak, total)
    far_back = lax.ppermute(far_part, "row", link_swap)
    near_part, dqt = near_row(qd, near, e, share, dqt)
    near_back = lax.ppermute(near_part, "row", chip_swap)
    mine = own_row(qd, own, e, share, dqt)
    return tuple(unpack(exchange(add_parts(mine, near_back, far_back))))


def solution(mesh):
    devices = mesh.devices
    if mesh.axis_names != ("head", "blk"):
        raise ValueError("mesh axes")
    heads = devices.shape[0]
    grid = Mesh(devices.reshape(heads, FRAMES, devices.shape[1] // FRAMES), ("head", "frame", "row"))
    tokens = P(("frame", "row", "head"), None)
    return jax.shard_map(
        per_device,
        mesh=grid,
        in_specs=(tokens,) * 5 + (P(("frame", "row"), None),),
        out_specs=(tokens,) * 3,
        check_vma=False,
    )
```

```python
import functools

import jax
import jax.numpy as jnp
from jax import lax
from jax.experimental import pallas as pl
from jax.experimental.pallas import tpu as pltpu
from jax.sharding import Mesh, PartitionSpec as P

HEADS = 16
DIM = 128
TILE = 128
COLS = 8
ROWS = 16
FRAMES = 2
GROUP = FRAMES * COLS
EXTRA = 8
NEAR_FLOPS = 2 * 10**9
OWN_FLOPS = 2 * 10**9
SECOND = 2 * TILE + EXTRA
BIG = 1e30
SCALE = DIM**-0.5
C = SCALE * 1.4426950408889634

F32 = jnp.float32
BF16 = jnp.bfloat16
VMEM_LIMIT = 20 * 1024 * 1024


def params(**kw):
    return pltpu.CompilerParams(vmem_limit_bytes=VMEM_LIMIT, **kw)


def small():
    return pltpu.CompilerParams(vmem_limit_bytes=8 * 1024 * 1024)


SMEM = pl.BlockSpec(memory_space=pltpu.SMEM)
VM = pl.BlockSpec(memory_space=pltpu.VMEM)
ANY = pl.BlockSpec(memory_space=pl.ANY)


CHUNKS = 2


def pack_first_kernel(k_ref, v_ref, out_ref, flat_ref, packed_ref, in_sem, out_sem):
    rows_in = TILE // CHUNKS
    refs = (k_ref, v_ref)

    def fetch(part, i):
        rows = pl.ds(i * rows_in, rows_in)
        return pltpu.make_async_copy(refs[part].at[rows, :], flat_ref.at[part, rows, :], in_sem.at[part, i])

    def send(part, i):
        rows = pl.ds(part * TILE + i * rows_in, rows_in)
        return pltpu.make_async_copy(packed_ref.at[:, rows, :], out_ref.at[:, rows, :], out_sem.at[part, i])

    for i in range(CHUNKS):
        for part in range(2):
            fetch(part, i).start()
    for i in range(CHUNKS):
        for part in range(2):
            fetch(part, i).wait()
            for h in range(HEADS):
                packed_ref[h, part * TILE + i * rows_in : part * TILE + (i + 1) * rows_in, :] = flat_ref[
                    part, i * rows_in : (i + 1) * rows_in, h * DIM : (h + 1) * DIM
                ]
            send(part, i).start()
    for i in range(CHUNKS):
        for part in range(2):
            send(part, i).wait()


def pack_first(keys, values):
    return pl.pallas_call(
        pack_first_kernel,
        in_specs=[ANY, ANY],
        out_specs=ANY,
        out_shape=jax.ShapeDtypeStruct((HEADS, 2 * TILE, DIM), BF16),
        scratch_shapes=[
            pltpu.VMEM((2, TILE, HEADS * DIM), BF16),
            pltpu.VMEM((HEADS, 2 * TILE, DIM), BF16),
            pltpu.SemaphoreType.DMA((2, CHUNKS)),
            pltpu.SemaphoreType.DMA((2, CHUNKS)),
        ],
        compiler_params=pltpu.CompilerParams(vmem_limit_bytes=58 * 1024 * 1024),
        cost_estimate=pl.CostEstimate(flops=0, bytes_accessed=2**21, transcendentals=0),
        name="pack_keys_values",
    )(keys, values)


def pack_second_kernel(w_ref, q_ref, g_ref, o_ref, m_ref, out_ref):
    mine = m_ref[pl.ds(w_ref[0], 1), :].astype(F32)
    rows = lax.broadcasted_iota(jnp.int32, (EXTRA, TILE), 0)
    for h in range(out_ref.shape[0]):
        cols = slice(h * DIM, (h + 1) * DIM)
        g = g_ref[:, cols]
        out_ref[h, :TILE, :] = q_ref[:, cols]
        out_ref[h, TILE : 2 * TILE, :] = g
        prod = g.astype(F32) * o_ref[:, cols].astype(F32)
        delta = jnp.sum(prod.T, axis=0, keepdims=True)
        high = delta.astype(BF16).astype(F32)
        extra = jnp.where(rows == 0, high, 0.0)
        extra = jnp.where(rows == 1, delta - high, extra)
        extra = jnp.where(rows == 2, mine[:, :TILE], extra)
        out_ref[h, 2 * TILE :, :] = jnp.where(rows == 3, mine[:, TILE:], extra).astype(BF16)


def pack_second(w, q, g, o, mask):
    step = 4
    block = pl.BlockSpec((TILE, step * DIM), lambda i: (0, i))
    return pl.pallas_call(
        pack_second_kernel,
        grid=(HEADS // step,),
        in_specs=[SMEM, block, block, block, pl.BlockSpec((COLS, 2 * TILE), lambda i: (0, 0))],
        out_specs=pl.BlockSpec((step, SECOND, DIM), lambda i: (i, 0, 0)),
        out_shape=jax.ShapeDtypeStruct((HEADS, SECOND, DIM), BF16),
        compiler_params=small(),
        cost_estimate=pl.CostEstimate(flops=2**20, bytes_accessed=5 * 2**19, transcendentals=0),
        name="pack_queries",
    )(w, q, g, o, mask)


def unpack_kernel(in_ref, q_ref, k_ref, v_ref, flat_ref, sem):
    rows_out = TILE // CHUNKS
    refs = (q_ref, k_ref, v_ref)

    def send(part, i):
        rows = pl.ds(i * rows_out, rows_out)
        return pltpu.make_async_copy(flat_ref.at[part, rows, :], refs[part].at[rows, :], sem.at[part, i])

    for part in range(3):
        for i in range(CHUNKS):
            for h in range(HEADS):
                flat_ref[part, i * rows_out : (i + 1) * rows_out, h * DIM : (h + 1) * DIM] = in_ref[
                    h, part * TILE + i * rows_out : part * TILE + (i + 1) * rows_out, :
                ]
            send(part, i).start()
    for part in range(3):
        for i in range(CHUNKS):
            send(part, i).wait()


def unpack(x):
    out = jax.ShapeDtypeStruct((TILE, HEADS * DIM), BF16)
    return pl.pallas_call(
        unpack_kernel,
        in_specs=[VM],
        out_specs=[ANY] * 3,
        out_shape=[out] * 3,
        scratch_shapes=[pltpu.VMEM((3, TILE, HEADS * DIM), BF16), pltpu.SemaphoreType.DMA((3, CHUNKS))],
        compiler_params=small(),
        cost_estimate=pl.CostEstimate(flops=0, bytes_accessed=3 * 2**20, transcendentals=0),
        name="unpack_grads",
    )(x)


def add_kernel(mine_ref, near_ref, far_ref, out_ref):
    out_ref[:, :TILE, :] = mine_ref[:, :TILE, :]
    for i in range(out_ref.shape[0]):
        far = far_ref[i * 2 * TILE : (i + 1) * 2 * TILE, :].astype(F32)
        total = mine_ref[i, TILE:, :].astype(F32) + near_ref[i].astype(F32) + far
        out_ref[i, TILE:, :] = total.astype(BF16)


def add_parts(mine, near, far):
    step = 4
    block = pl.BlockSpec((step, 2 * TILE, DIM), lambda i: (i, 0, 0))
    wide = pl.BlockSpec((step, 3 * TILE, DIM), lambda i: (i, 0, 0))
    return pl.pallas_call(
        add_kernel,
        grid=(GROUP // step,),
        in_specs=[wide, block, pl.BlockSpec((step * 2 * TILE, DIM), lambda i: (i, 0))],
        out_specs=wide,
        out_shape=jax.ShapeDtypeStruct((GROUP, 3 * TILE, DIM), BF16),
        compiler_params=small(),
        cost_estimate=pl.CostEstimate(flops=2**20, bytes_accessed=5 * 2**20, transcendentals=0),
        name="add_parts",
    )(mine, near, far)


def dot_nt(a, b):
    return lax.dot_general(a, b, (((1,), (1,)), ((), ())), preferred_element_type=F32)


def dot_nn(a, b):
    return lax.dot_general(a, b, (((1,), (0,)), ((), ())), preferred_element_type=F32)


EDGE_LEFT = ((1, 0, True, False), (2, 1, True, False))
EDGE_RIGHT = ((0, COLS - 2, False, True), (1, COLS - 1, False, True))


def inner_steps(w):
    return ((0, w - 1, False, True), (1, w, False, False), (2, w + 1, True, False))


def sweep(body):
    body(0, EDGE_LEFT)

    def inner(w, carry):
        body(w, inner_steps(w))
        return carry

    lax.fori_loop(1, COLS - 1, inner, 0)
    body(COLS - 1, EDGE_RIGHT)


def both(ref, col, part):
    rows = slice(part * TILE, (part + 1) * TILE)
    return jnp.concatenate([ref[col, rows, :], ref[COLS + col, rows, :]], axis=0)


def penalties(rows_ref, m_ref, unit, w, place):
    wanted = w + place - 1
    col = jnp.clip(wanted, 0, COLS - 1)
    inside = (rows_ref[unit + 3] != 0) & (wanted == col)
    found = []
    for key_frame in range(FRAMES):
        at = key_frame * TILE + rows_ref[unit] * COLS + col
        found.append(
            [
                jnp.where((m_ref[frame * COLS + w, at] != 0) & inside, 0.0, BIG).astype(F32)
                for frame in range(FRAMES)
            ]
        )
    return found


def shifted(x, pens, sign):
    return jnp.concatenate([x[:, :TILE] + sign * pens[0], x[:, TILE:] + sign * pens[1]], axis=1)


def exponentials(piece, level):
    e = jnp.exp2(piece.reshape(TILE // 8, 8, 2 * TILE) * C - level[None])
    return e.reshape(TILE, 2 * TILE), jnp.sum(e, axis=0)


def score(rows_ref, m_ref, unit, kv_ref, q, w, s_ref, top, wide):
    cols = [jnp.clip(w + place - 1, 0, COLS - 1) for place in range(3)]
    keys = [both(kv_ref, col, 0) for col in cols]
    if wide:
        scores = dot_nt(jnp.concatenate(keys, axis=0), q)
        scores = [scores[2 * TILE * place : 2 * TILE * (place + 1)] for place in range(3)]
    else:
        scores = [dot_nt(key, q) for key in keys]
    for place in range(3):
        pens = penalties(rows_ref, m_ref, unit, w, place)
        for frame in range(FRAMES):
            piece = scores[place][frame * TILE : (frame + 1) * TILE]
            s_ref[place, frame * TILE : (frame + 1) * TILE, :] = piece
            top = jnp.maximum(top, shifted(fold(piece, jnp.max), pens[frame], -1.0))
    return top


def spread(x):
    return jnp.broadcast_to(x, (8, 2 * TILE))


def fold(x, op):
    return op(x.reshape(TILE // 8, 8, 2 * TILE), axis=0)


def query_side(qd_ref, w):
    q = both(qd_ref, w, 0)
    g = both(qd_ref, w, 1)
    delta = []
    for frame in range(FRAMES):
        extra = qd_ref[frame * COLS + w, 2 * TILE :, :].astype(F32)
        delta.append(extra[0:1, :] + extra[1:2, :])
    return q, g, jnp.concatenate(delta, axis=1)


def column_grads(kv_ref, kt_ref, dk_ref, dv_ref, out_ref, at, prob, q, g, delta, steps):
    dprob = dot_nt(jnp.concatenate([both(kv_ref, col, 1) for _, col, _, _ in steps], axis=0), g)
    dscore = (prob * (dprob - delta)).astype(BF16)
    dv = dot_nn(prob.astype(BF16), g)
    dk = dot_nn(dscore, q)
    turned_keys = []
    for i, (_, col, first, last) in enumerate(steps):
        if first:
            kt_ref[col] = jnp.concatenate([kv_ref[col, :TILE, :].T, kv_ref[COLS + col, :TILE, :].T], axis=1)
        turned_keys.append(kt_ref[col])
        for frame in range(FRAMES):
            rows = slice((FRAMES * i + frame) * TILE, (FRAMES * i + frame + 1) * TILE)
            tile = frame * COLS + col
            dv_here, dk_here = dv[rows], dk[rows]
            if not first:
                dv_here += dv_ref[tile]
                dk_here += dk_ref[tile]
            if last and at is None:
                out_ref[pl.ds(tile * 2 * TILE, TILE), :] = (dk_here * SCALE).astype(BF16)
                out_ref[pl.ds(tile * 2 * TILE + TILE, TILE), :] = dv_here.astype(BF16)
            elif last:
                out_ref[tile, at * TILE : (at + 1) * TILE, :] = (dk_here * SCALE).astype(BF16)
                out_ref[tile, (at + 1) * TILE : (at + 2) * TILE, :] = dv_here.astype(BF16)
            else:
                dv_ref[tile] = dv_here
                dk_ref[tile] = dk_here
    return dot_nn(jnp.concatenate(turned_keys, axis=1), dscore)


def early_kernel(rows_ref, m_ref, qd_ref, own_ref, near_ref, e_ref, peak_ref, total_ref, even_ref, odd_ref):
    def scores(w, s_ref):
        q = both(qd_ref, w, 0)
        top = jnp.full((8, 2 * TILE), -BIG, F32)
        for unit, kv_ref in enumerate((near_ref, own_ref)):
            top = score(rows_ref, m_ref, unit, kv_ref, q, w, s_ref.at[unit], top, True)
        peak_ref[w] = spread(jnp.max(top, axis=0, keepdims=True))

    def weigh(w, s_ref):
        level = peak_ref[w] * C
        total = jnp.zeros((8, 2 * TILE), F32)
        for unit in range(2):
            for place in range(3):
                pens = penalties(rows_ref, m_ref, unit, w, place)
                for frame in range(FRAMES):
                    below = shifted(level, pens[frame], 1.0)
                    for part in range(4):
                        rows = slice(frame * TILE + part * 32, frame * TILE + part * 32 + 32)
                        x = s_ref[unit, place, rows, :].reshape(4, 8, 2 * TILE)
                        e = jnp.exp2(x * C - below[None])
                        e_ref[w, unit, place, rows, :] = e.reshape(32, 2 * TILE).astype(BF16)
                        total += (e[0] + e[1]) + (e[2] + e[3])
        total_ref[w] = spread(jnp.sum(total, axis=0, keepdims=True))

    def two(i, carry):
        w = 2 * i
        scores(w + 1, odd_ref)
        weigh(w, even_ref)
        scores(jnp.minimum(w + 2, COLS - 1), even_ref)
        weigh(w + 1, odd_ref)
        return carry

    scores(0, even_ref)
    lax.fori_loop(0, COLS // 2, two, 0)


def far_kernel(
    rows_ref, m_ref, qd_ref, far_ref, peak_ref, total_ref, part_ref, share_ref, dqt_ref,
    even_ref, odd_ref, kt_ref, dk_ref, dv_ref,
):
    part_ref[GROUP * 2 * TILE :, :] = jnp.zeros((EXTRA, DIM), BF16)

    def weigh(w, s_ref):
        early = peak_ref[w]
        top = score(rows_ref, m_ref, 2, far_ref, both(qd_ref, w, 0), w, s_ref, early, False)
        peak = spread(jnp.max(top, axis=0, keepdims=True))
        total = jnp.zeros((8, 2 * TILE), F32)
        for place in range(3):
            pens = penalties(rows_ref, m_ref, 2, w, place)
            for frame in range(FRAMES):
                below = shifted(peak * C, pens[frame], 1.0)
                for part in range(4):
                    rows = slice(frame * TILE + part * 32, frame * TILE + part * 32 + 32)
                    x = s_ref[place, rows, :].reshape(4, 8, 2 * TILE)
                    e = jnp.exp2(x * C - below[None])
                    s_ref[place, rows, :] = e.reshape(32, 2 * TILE)
                    total += (e[0] + e[1]) + (e[2] + e[3])
        shrink = jnp.exp2((early - peak) * C)
        share = 1.0 / (jnp.sum(total, axis=0, keepdims=True) + total_ref[w] * shrink)
        share_ref[w] = shrink * share
        return share[0:1, :]

    def grads(w, share, s_ref, steps):
        q, g, delta = query_side(qd_ref, w)
        prob = jnp.concatenate([s_ref[place] for place, _, _, _ in steps], axis=0) * share
        dqt_ref[w] = column_grads(far_ref, kt_ref, dk_ref, dv_ref, part_ref, None, prob, q, g, delta, steps)

    edge = COLS - 1
    share = weigh(0, even_ref)
    later = weigh(1, odd_ref)
    grads(0, share, even_ref, EDGE_LEFT)

    def two(i, share):
        w = 2 * i + 1
        later = weigh(w + 1, even_ref)
        grads(w, share, odd_ref, inner_steps(w))
        share = weigh(w + 2, odd_ref)
        grads(w + 1, later, even_ref, inner_steps(w + 1))
        return share

    share = lax.fori_loop(0, (COLS - 2) // 2, two, later)
    grads(edge, share, odd_ref, EDGE_RIGHT)


def row_kernel(unit, qd_ref, kv_ref, e_ref, share_ref, dqt_ref, out_ref, sum_ref, kt_ref, dk_ref, dv_ref):
    def body(w, steps):
        q, g, delta = query_side(qd_ref, w)
        share = share_ref[w, 0:1, :]
        prob = jnp.concatenate([e_ref[w, unit, place] for place, _, _, _ in steps], axis=0).astype(F32) * share
        dqt = dqt_ref[w] + column_grads(kv_ref, kt_ref, dk_ref, dv_ref, out_ref, unit, prob, q, g, delta, steps)
        if unit == 1:
            dq = (dqt.T * SCALE).astype(BF16)
            out_ref[w, :TILE, :] = dq[:TILE]
            out_ref[COLS + w, :TILE, :] = dq[TILE:]
        else:
            sum_ref[w] = dqt

    sweep(body)


def near_kernel(qd_ref, kv_ref, e_ref, share_ref, dqt_ref, out_ref, sum_ref, kt_ref, dk_ref, dv_ref):
    row_kernel(0, qd_ref, kv_ref, e_ref, share_ref, dqt_ref, out_ref, sum_ref, kt_ref, dk_ref, dv_ref)


def own_kernel(qd_ref, kv_ref, e_ref, share_ref, dqt_ref, out_ref, kt_ref, dk_ref, dv_ref):
    row_kernel(1, qd_ref, kv_ref, e_ref, share_ref, dqt_ref, out_ref, None, kt_ref, dk_ref, dv_ref)


def acc():
    return pltpu.VMEM((GROUP, TILE, DIM), F32)


def turned():
    return pltpu.VMEM((COLS, DIM, 2 * TILE), BF16)


ROWS_OF = jax.ShapeDtypeStruct((COLS, 8, 2 * TILE), F32)
PART = jax.ShapeDtypeStruct((GROUP, 2 * TILE, DIM), BF16)
FAR_PART = jax.ShapeDtypeStruct((GROUP * 2 * TILE + EXTRA, DIM), BF16)


def early(rows, live, qd, own, near):
    return pl.pallas_call(
        early_kernel,
        in_specs=[SMEM, SMEM, VM, VM, VM],
        out_specs=[VM, VM, VM],
        out_shape=[jax.ShapeDtypeStruct((COLS, 2, 3, 2 * TILE, 2 * TILE), BF16), ROWS_OF, ROWS_OF],
        scratch_shapes=[pltpu.VMEM((2, 3, 2 * TILE, 2 * TILE), F32)] * 2,
        compiler_params=params(),
        cost_estimate=pl.CostEstimate(flops=2 * 10**9, bytes_accessed=3 * 2**20, transcendentals=3 * 10**6),
        name="near_and_own_scores",
    )(rows, live, qd, own, near)


def far_row(rows, live, qd, far, peak, total):
    return pl.pallas_call(
        far_kernel,
        in_specs=[SMEM, SMEM, VM, VM, VM, VM],
        out_specs=[VM, VM, VM],
        out_shape=[FAR_PART, ROWS_OF, jax.ShapeDtypeStruct((COLS, DIM, 2 * TILE), F32)],
        scratch_shapes=[pltpu.VMEM((3, 2 * TILE, 2 * TILE), F32)] * 2 + [turned(), acc(), acc()],
        compiler_params=params(),
        cost_estimate=pl.CostEstimate(flops=2 * 10**9, bytes_accessed=2**22, transcendentals=2 * 10**6),
        name="far_row",
    )(rows, live, qd, far, peak, total)


SUMS = jax.ShapeDtypeStruct((COLS, DIM, 2 * TILE), F32)


def near_row(qd, near, e, share, dqt):
    return pl.pallas_call(
        near_kernel,
        in_specs=[VM] * 5,
        out_specs=[VM, VM],
        out_shape=[PART, SUMS],
        scratch_shapes=[turned(), acc(), acc()],
        compiler_params=params(),
        cost_estimate=pl.CostEstimate(flops=NEAR_FLOPS, bytes_accessed=2**22, transcendentals=0),
        name="near_row",
    )(qd, near, e, share, dqt)


def own_row(qd, own, e, share, dqt):
    return pl.pallas_call(
        own_kernel,
        in_specs=[VM] * 5,
        out_specs=VM,
        out_shape=jax.ShapeDtypeStruct((GROUP, 3 * TILE, DIM), BF16),
        scratch_shapes=[turned(), acc(), acc()],
        compiler_params=params(),
        cost_estimate=pl.CostEstimate(flops=OWN_FLOPS, bytes_accessed=2**22, transcendentals=0),
        name="own_row",
    )(qd, own, e, share, dqt)


def per_device(queries, keys, values, d_out, saved_out, mask):
    group = ("frame", "head")
    row = lax.axis_index("row")
    is_even = lax.rem(row, 2) == 0
    chip_swap = [(i, i ^ 1) for i in range(ROWS)]
    link_swap = [(i, i + 1) for i in range(1, ROWS - 1, 2)] + [(i + 1, i) for i in range(1, ROWS - 1, 2)]

    def exchange(x):
        return lax.all_to_all(x, group, split_axis=0, concat_axis=0, tiled=True)

    w = lax.axis_index("head").astype(jnp.int32).reshape(1)
    own = exchange(pack_first(keys, values))
    second = pack_second(w, queries, d_out, saved_out, mask)
    own, second = lax.optimization_barrier((own, second))
    qd = exchange(second)
    far = lax.ppermute(own, "row", link_swap)
    near = lax.ppermute(own, "row", chip_swap)

    far_index = jnp.where(is_even, row - 1, row + 1)
    near_index = jnp.where(is_even, row + 1, row - 1)
    rows = jnp.stack([near_index, row, far_index]).astype(jnp.int32)
    inside = ((rows >= 0) & (rows < ROWS)).astype(jnp.int32)
    rows = jnp.concatenate([jnp.clip(rows, 0, ROWS - 1), inside])
    live = qd[:, 2 * TILE + 2 : 2 * TILE + 4, :].astype(jnp.int32).reshape(GROUP, 2 * TILE)

    e, peak, total = early(rows, live, qd, own, near)
    far_part, share, dqt = far_row(rows, live, qd, far, peak, total)
    far_back = lax.ppermute(far_part, "row", link_swap)
    near_part, dqt = near_row(qd, near, e, share, dqt)
    near_back = lax.ppermute(near_part, "row", chip_swap)
    mine = own_row(qd, own, e, share, dqt)
    return tuple(unpack(exchange(add_parts(mine, near_back, far_back))))


def solution(mesh):
    devices = mesh.devices
    if mesh.axis_names != ("head", "blk"):
        raise ValueError("mesh axes")
    heads = devices.shape[0]
    grid = Mesh(devices.reshape(heads, FRAMES, devices.shape[1] // FRAMES), ("head", "frame", "row"))
    tokens = P(("frame", "row", "head"), None)
    return jax.shard_map(
        per_device,
        mesh=grid,
        in_specs=(tokens,) * 5 + (P(("frame", "row"), None),),
        out_specs=(tokens,) * 3,
        check_vma=False,
    )
```

```python
import functools

import jax
import jax.numpy as jnp
from jax import lax
from jax.experimental import pallas as pl
from jax.experimental.pallas import tpu as pltpu
from jax.sharding import Mesh, PartitionSpec as P

HEADS = 16
DIM = 128
TILE = 128
COLS = 8
ROWS = 16
FRAMES = 2
GROUP = FRAMES * COLS
EXTRA = 8
NEAR_FLOPS = 2 * 10**9
OWN_FLOPS = 2 * 10**9
SECOND = 2 * TILE + EXTRA
BIG = 1e30
SCALE = DIM**-0.5
C = SCALE * 1.4426950408889634

F32 = jnp.float32
BF16 = jnp.bfloat16
VMEM_LIMIT = 20 * 1024 * 1024


def params(**kw):
    return pltpu.CompilerParams(vmem_limit_bytes=VMEM_LIMIT, **kw)


def small():
    return pltpu.CompilerParams(vmem_limit_bytes=8 * 1024 * 1024)


SMEM = pl.BlockSpec(memory_space=pltpu.SMEM)
VM = pl.BlockSpec(memory_space=pltpu.VMEM)
ANY = pl.BlockSpec(memory_space=pl.ANY)


CHUNKS = 2


def pack_first_kernel(k_ref, v_ref, out_ref, flat_ref, packed_ref, in_sem, out_sem):
    rows_in = TILE // CHUNKS
    refs = (k_ref, v_ref)

    def fetch(part, i):
        rows = pl.ds(i * rows_in, rows_in)
        return pltpu.make_async_copy(refs[part].at[rows, :], flat_ref.at[part, rows, :], in_sem.at[part, i])

    def send(part, i):
        rows = pl.ds(part * TILE + i * rows_in, rows_in)
        return pltpu.make_async_copy(packed_ref.at[:, rows, :], out_ref.at[:, rows, :], out_sem.at[part, i])

    for i in range(CHUNKS):
        for part in range(2):
            fetch(part, i).start()
    for i in range(CHUNKS):
        for part in range(2):
            fetch(part, i).wait()
            for h in range(HEADS):
                packed_ref[h, part * TILE + i * rows_in : part * TILE + (i + 1) * rows_in, :] = flat_ref[
                    part, i * rows_in : (i + 1) * rows_in, h * DIM : (h + 1) * DIM
                ]
            send(part, i).start()
    for i in range(CHUNKS):
        for part in range(2):
            send(part, i).wait()


def pack_first(keys, values):
    return pl.pallas_call(
        pack_first_kernel,
        in_specs=[ANY, ANY],
        out_specs=ANY,
        out_shape=jax.ShapeDtypeStruct((HEADS, 2 * TILE, DIM), BF16),
        scratch_shapes=[
            pltpu.VMEM((2, TILE, HEADS * DIM), BF16),
            pltpu.VMEM((HEADS, 2 * TILE, DIM), BF16),
            pltpu.SemaphoreType.DMA((2, CHUNKS)),
            pltpu.SemaphoreType.DMA((2, CHUNKS)),
        ],
        compiler_params=pltpu.CompilerParams(vmem_limit_bytes=58 * 1024 * 1024),
        cost_estimate=pl.CostEstimate(flops=0, bytes_accessed=2**21, transcendentals=0),
        name="pack_keys_values",
    )(keys, values)


def pack_second_kernel(w_ref, q_ref, g_ref, o_ref, m_ref, out_ref):
    mine = m_ref[pl.ds(w_ref[0], 1), :].astype(F32)
    rows = lax.broadcasted_iota(jnp.int32, (EXTRA, TILE), 0)
    for h in range(out_ref.shape[0]):
        cols = slice(h * DIM, (h + 1) * DIM)
        g = g_ref[:, cols]
        out_ref[h, :TILE, :] = q_ref[:, cols]
        out_ref[h, TILE : 2 * TILE, :] = g
        prod = g.astype(F32) * o_ref[:, cols].astype(F32)
        delta = jnp.sum(prod.T, axis=0, keepdims=True)
        high = delta.astype(BF16).astype(F32)
        extra = jnp.where(rows == 0, high, 0.0)
        extra = jnp.where(rows == 1, delta - high, extra)
        extra = jnp.where(rows == 2, mine[:, :TILE], extra)
        out_ref[h, 2 * TILE :, :] = jnp.where(rows == 3, mine[:, TILE:], extra).astype(BF16)


def pack_second(w, q, g, o, mask):
    step = 4
    block = pl.BlockSpec((TILE, step * DIM), lambda i: (0, i))
    return pl.pallas_call(
        pack_second_kernel,
        grid=(HEADS // step,),
        in_specs=[SMEM, block, block, block, pl.BlockSpec((COLS, 2 * TILE), lambda i: (0, 0))],
        out_specs=pl.BlockSpec((step, SECOND, DIM), lambda i: (i, 0, 0)),
        out_shape=jax.ShapeDtypeStruct((HEADS, SECOND, DIM), BF16),
        compiler_params=small(),
        cost_estimate=pl.CostEstimate(flops=2**20, bytes_accessed=5 * 2**19, transcendentals=0),
        name="pack_queries",
    )(w, q, g, o, mask)


def unpack_kernel(in_ref, q_ref, k_ref, v_ref, flat_ref, sem):
    rows_out = TILE // CHUNKS
    refs = (q_ref, k_ref, v_ref)

    def send(part, i):
        rows = pl.ds(i * rows_out, rows_out)
        return pltpu.make_async_copy(flat_ref.at[part, rows, :], refs[part].at[rows, :], sem.at[part, i])

    for part in range(3):
        for i in range(CHUNKS):
            for h in range(HEADS):
                flat_ref[part, i * rows_out : (i + 1) * rows_out, h * DIM : (h + 1) * DIM] = in_ref[
                    h, part * TILE + i * rows_out : part * TILE + (i + 1) * rows_out, :
                ]
            send(part, i).start()
    for part in range(3):
        for i in range(CHUNKS):
            send(part, i).wait()


def unpack(x):
    out = jax.ShapeDtypeStruct((TILE, HEADS * DIM), BF16)
    return pl.pallas_call(
        unpack_kernel,
        in_specs=[VM],
        out_specs=[ANY] * 3,
        out_shape=[out] * 3,
        scratch_shapes=[pltpu.VMEM((3, TILE, HEADS * DIM), BF16), pltpu.SemaphoreType.DMA((3, CHUNKS))],
        compiler_params=small(),
        cost_estimate=pl.CostEstimate(flops=0, bytes_accessed=3 * 2**20, transcendentals=0),
        name="unpack_grads",
    )(x)


def add_kernel(mine_ref, near_ref, far_ref, out_ref):
    out_ref[:, :TILE, :] = mine_ref[:, :TILE, :]
    for i in range(out_ref.shape[0]):
        far = far_ref[i * 2 * TILE : (i + 1) * 2 * TILE, :].astype(F32)
        total = mine_ref[i, TILE:, :].astype(F32) + near_ref[i].astype(F32) + far
        out_ref[i, TILE:, :] = total.astype(BF16)


def add_parts(mine, near, far):
    step = 8
    block = pl.BlockSpec((step, 2 * TILE, DIM), lambda i: (i, 0, 0))
    wide = pl.BlockSpec((step, 3 * TILE, DIM), lambda i: (i, 0, 0))
    return pl.pallas_call(
        add_kernel,
        grid=(GROUP // step,),
        in_specs=[wide, block, pl.BlockSpec((step * 2 * TILE, DIM), lambda i: (i, 0))],
        out_specs=wide,
        out_shape=jax.ShapeDtypeStruct((GROUP, 3 * TILE, DIM), BF16),
        compiler_params=small(),
        cost_estimate=pl.CostEstimate(flops=2**20, bytes_accessed=5 * 2**20, transcendentals=0),
        name="add_parts",
    )(mine, near, far)


def dot_nt(a, b):
    return lax.dot_general(a, b, (((1,), (1,)), ((), ())), preferred_element_type=F32)


def dot_nn(a, b):
    return lax.dot_general(a, b, (((1,), (0,)), ((), ())), preferred_element_type=F32)


EDGE_LEFT = ((1, 0, True, False), (2, 1, True, False))
EDGE_RIGHT = ((0, COLS - 2, False, True), (1, COLS - 1, False, True))


def inner_steps(w):
    return ((0, w - 1, False, True), (1, w, False, False), (2, w + 1, True, False))


def sweep(body):
    body(0, EDGE_LEFT)

    def inner(w, carry):
        body(w, inner_steps(w))
        return carry

    lax.fori_loop(1, COLS - 1, inner, 0)
    body(COLS - 1, EDGE_RIGHT)


def both(ref, col, part):
    rows = slice(part * TILE, (part + 1) * TILE)
    return jnp.concatenate([ref[col, rows, :], ref[COLS + col, rows, :]], axis=0)


def penalties(rows_ref, m_ref, unit, w, place):
    wanted = w + place - 1
    col = jnp.clip(wanted, 0, COLS - 1)
    inside = (rows_ref[unit + 3] != 0) & (wanted == col)
    found = []
    for key_frame in range(FRAMES):
        at = key_frame * TILE + rows_ref[unit] * COLS + col
        found.append(
            [
                jnp.where((m_ref[frame * COLS + w, at] != 0) & inside, 0.0, BIG).astype(F32)
                for frame in range(FRAMES)
            ]
        )
    return found


def shifted(x, pens, sign):
    return jnp.concatenate([x[:, :TILE] + sign * pens[0], x[:, TILE:] + sign * pens[1]], axis=1)


def exponentials(piece, level):
    e = jnp.exp2(piece.reshape(TILE // 8, 8, 2 * TILE) * C - level[None])
    return e.reshape(TILE, 2 * TILE), jnp.sum(e, axis=0)


def score(rows_ref, m_ref, unit, kv_ref, q, w, s_ref, top, wide):
    cols = [jnp.clip(w + place - 1, 0, COLS - 1) for place in range(3)]
    keys = [both(kv_ref, col, 0) for col in cols]
    if wide:
        scores = dot_nt(jnp.concatenate(keys, axis=0), q)
        scores = [scores[2 * TILE * place : 2 * TILE * (place + 1)] for place in range(3)]
    else:
        scores = [dot_nt(key, q) for key in keys]
    for place in range(3):
        pens = penalties(rows_ref, m_ref, unit, w, place)
        for frame in range(FRAMES):
            piece = scores[place][frame * TILE : (frame + 1) * TILE]
            s_ref[place, frame * TILE : (frame + 1) * TILE, :] = piece
            top = jnp.maximum(top, shifted(fold(piece, jnp.max), pens[frame], -1.0))
    return top


def spread(x):
    return jnp.broadcast_to(x, (8, 2 * TILE))


def fold(x, op):
    return op(x.reshape(TILE // 8, 8, 2 * TILE), axis=0)


def query_side(qd_ref, w):
    q = both(qd_ref, w, 0)
    g = both(qd_ref, w, 1)
    delta = []
    for frame in range(FRAMES):
        extra = qd_ref[frame * COLS + w, 2 * TILE :, :].astype(F32)
        delta.append(extra[0:1, :] + extra[1:2, :])
    return q, g, jnp.concatenate(delta, axis=1)


def column_grads(kv_ref, kt_ref, dk_ref, dv_ref, out_ref, at, prob, q, g, delta, steps):
    dprob = dot_nt(jnp.concatenate([both(kv_ref, col, 1) for _, col, _, _ in steps], axis=0), g)
    dscore = (prob * (dprob - delta)).astype(BF16)
    dv = dot_nn(prob.astype(BF16), g)
    dk = dot_nn(dscore, q)
    turned_keys = []
    for i, (_, col, first, last) in enumerate(steps):
        if first:
            kt_ref[col] = jnp.concatenate([kv_ref[col, :TILE, :].T, kv_ref[COLS + col, :TILE, :].T], axis=1)
        turned_keys.append(kt_ref[col])
        for frame in range(FRAMES):
            rows = slice((FRAMES * i + frame) * TILE, (FRAMES * i + frame + 1) * TILE)
            tile = frame * COLS + col
            dv_here, dk_here = dv[rows], dk[rows]
            if not first:
                dv_here += dv_ref[tile]
                dk_here += dk_ref[tile]
            if last and at is None:
                out_ref[pl.ds(tile * 2 * TILE, TILE), :] = (dk_here * SCALE).astype(BF16)
                out_ref[pl.ds(tile * 2 * TILE + TILE, TILE), :] = dv_here.astype(BF16)
            elif last:
                out_ref[tile, at * TILE : (at + 1) * TILE, :] = (dk_here * SCALE).astype(BF16)
                out_ref[tile, (at + 1) * TILE : (at + 2) * TILE, :] = dv_here.astype(BF16)
            else:
                dv_ref[tile] = dv_here
                dk_ref[tile] = dk_here
    return dot_nn(jnp.concatenate(turned_keys, axis=1), dscore)


def early_kernel(rows_ref, m_ref, qd_ref, own_ref, near_ref, e_ref, peak_ref, total_ref, even_ref, odd_ref):
    def scores(w, s_ref):
        q = both(qd_ref, w, 0)
        top = jnp.full((8, 2 * TILE), -BIG, F32)
        for unit, kv_ref in enumerate((near_ref, own_ref)):
            top = score(rows_ref, m_ref, unit, kv_ref, q, w, s_ref.at[unit], top, True)
        peak_ref[w] = spread(jnp.max(top, axis=0, keepdims=True))

    def weigh(w, s_ref):
        level = peak_ref[w] * C
        total = jnp.zeros((8, 2 * TILE), F32)
        for unit in range(2):
            for place in range(3):
                pens = penalties(rows_ref, m_ref, unit, w, place)
                for frame in range(FRAMES):
                    below = shifted(level, pens[frame], 1.0)
                    for part in range(4):
                        rows = slice(frame * TILE + part * 32, frame * TILE + part * 32 + 32)
                        x = s_ref[unit, place, rows, :].reshape(4, 8, 2 * TILE)
                        e = jnp.exp2(x * C - below[None])
                        e_ref[w, unit, place, rows, :] = e.reshape(32, 2 * TILE).astype(BF16)
                        total += (e[0] + e[1]) + (e[2] + e[3])
        total_ref[w] = spread(jnp.sum(total, axis=0, keepdims=True))

    def two(i, carry):
        w = 2 * i
        scores(w + 1, odd_ref)
        weigh(w, even_ref)
        scores(jnp.minimum(w + 2, COLS - 1), even_ref)
        weigh(w + 1, odd_ref)
        return carry

    scores(0, even_ref)
    lax.fori_loop(0, COLS // 2, two, 0)


def far_kernel(
    rows_ref, m_ref, qd_ref, far_ref, peak_ref, total_ref, part_ref, share_ref, dqt_ref,
    even_ref, odd_ref, kt_ref, dk_ref, dv_ref,
):
    part_ref[GROUP * 2 * TILE :, :] = jnp.zeros((EXTRA, DIM), BF16)

    def weigh(w, s_ref):
        early = peak_ref[w]
        top = score(rows_ref, m_ref, 2, far_ref, both(qd_ref, w, 0), w, s_ref, early, False)
        peak = spread(jnp.max(top, axis=0, keepdims=True))
        total = jnp.zeros((8, 2 * TILE), F32)
        for place in range(3):
            pens = penalties(rows_ref, m_ref, 2, w, place)
            for frame in range(FRAMES):
                below = shifted(peak * C, pens[frame], 1.0)
                for part in range(4):
                    rows = slice(frame * TILE + part * 32, frame * TILE + part * 32 + 32)
                    x = s_ref[place, rows, :].reshape(4, 8, 2 * TILE)
                    e = jnp.exp2(x * C - below[None])
                    s_ref[place, rows, :] = e.reshape(32, 2 * TILE)
                    total += (e[0] + e[1]) + (e[2] + e[3])
        shrink = jnp.exp2((early - peak) * C)
        share = 1.0 / (jnp.sum(total, axis=0, keepdims=True) + total_ref[w] * shrink)
        share_ref[w] = shrink * share
        return share[0:1, :]

    def grads(w, share, s_ref, steps):
        q, g, delta = query_side(qd_ref, w)
        prob = jnp.concatenate([s_ref[place] for place, _, _, _ in steps], axis=0) * share
        dqt_ref[w] = column_grads(far_ref, kt_ref, dk_ref, dv_ref, part_ref, None, prob, q, g, delta, steps)

    edge = COLS - 1
    share = weigh(0, even_ref)
    later = weigh(1, odd_ref)
    grads(0, share, even_ref, EDGE_LEFT)

    def two(i, share):
        w = 2 * i + 1
        later = weigh(w + 1, even_ref)
        grads(w, share, odd_ref, inner_steps(w))
        share = weigh(w + 2, odd_ref)
        grads(w + 1, later, even_ref, inner_steps(w + 1))
        return share

    share = lax.fori_loop(0, (COLS - 2) // 2, two, later)
    grads(edge, share, odd_ref, EDGE_RIGHT)


def row_kernel(unit, qd_ref, kv_ref, e_ref, share_ref, dqt_ref, out_ref, sum_ref, kt_ref, dk_ref, dv_ref):
    def body(w, steps):
        q, g, delta = query_side(qd_ref, w)
        share = share_ref[w, 0:1, :]
        prob = jnp.concatenate([e_ref[w, unit, place] for place, _, _, _ in steps], axis=0).astype(F32) * share
        dqt = dqt_ref[w] + column_grads(kv_ref, kt_ref, dk_ref, dv_ref, out_ref, unit, prob, q, g, delta, steps)
        if unit == 1:
            dq = (dqt.T * SCALE).astype(BF16)
            out_ref[w, :TILE, :] = dq[:TILE]
            out_ref[COLS + w, :TILE, :] = dq[TILE:]
        else:
            sum_ref[w] = dqt

    sweep(body)


def near_kernel(qd_ref, kv_ref, e_ref, share_ref, dqt_ref, out_ref, sum_ref, kt_ref, dk_ref, dv_ref):
    row_kernel(0, qd_ref, kv_ref, e_ref, share_ref, dqt_ref, out_ref, sum_ref, kt_ref, dk_ref, dv_ref)


def own_kernel(qd_ref, kv_ref, e_ref, share_ref, dqt_ref, out_ref, kt_ref, dk_ref, dv_ref):
    row_kernel(1, qd_ref, kv_ref, e_ref, share_ref, dqt_ref, out_ref, None, kt_ref, dk_ref, dv_ref)


def acc():
    return pltpu.VMEM((GROUP, TILE, DIM), F32)


def turned():
    return pltpu.VMEM((COLS, DIM, 2 * TILE), BF16)


ROWS_OF = jax.ShapeDtypeStruct((COLS, 8, 2 * TILE), F32)
PART = jax.ShapeDtypeStruct((GROUP, 2 * TILE, DIM), BF16)
FAR_PART = jax.ShapeDtypeStruct((GROUP * 2 * TILE + EXTRA, DIM), BF16)


def early(rows, live, qd, own, near):
    return pl.pallas_call(
        early_kernel,
        in_specs=[SMEM, SMEM, VM, VM, VM],
        out_specs=[VM, VM, VM],
        out_shape=[jax.ShapeDtypeStruct((COLS, 2, 3, 2 * TILE, 2 * TILE), BF16), ROWS_OF, ROWS_OF],
        scratch_shapes=[pltpu.VMEM((2, 3, 2 * TILE, 2 * TILE), F32)] * 2,
        compiler_params=params(),
        cost_estimate=pl.CostEstimate(flops=2 * 10**9, bytes_accessed=3 * 2**20, transcendentals=3 * 10**6),
        name="near_and_own_scores",
    )(rows, live, qd, own, near)


def far_row(rows, live, qd, far, peak, total):
    return pl.pallas_call(
        far_kernel,
        in_specs=[SMEM, SMEM, VM, VM, VM, VM],
        out_specs=[VM, VM, VM],
        out_shape=[FAR_PART, ROWS_OF, jax.ShapeDtypeStruct((COLS, DIM, 2 * TILE), F32)],
        scratch_shapes=[pltpu.VMEM((3, 2 * TILE, 2 * TILE), F32)] * 2 + [turned(), acc(), acc()],
        compiler_params=params(),
        cost_estimate=pl.CostEstimate(flops=2 * 10**9, bytes_accessed=2**22, transcendentals=2 * 10**6),
        name="far_row",
    )(rows, live, qd, far, peak, total)


SUMS = jax.ShapeDtypeStruct((COLS, DIM, 2 * TILE), F32)


def near_row(qd, near, e, share, dqt):
    return pl.pallas_call(
        near_kernel,
        in_specs=[VM] * 5,
        out_specs=[VM, VM],
        out_shape=[PART, SUMS],
        scratch_shapes=[turned(), acc(), acc()],
        compiler_params=params(),
        cost_estimate=pl.CostEstimate(flops=NEAR_FLOPS, bytes_accessed=2**22, transcendentals=0),
        name="near_row",
    )(qd, near, e, share, dqt)


def own_row(qd, own, e, share, dqt):
    return pl.pallas_call(
        own_kernel,
        in_specs=[VM] * 5,
        out_specs=VM,
        out_shape=jax.ShapeDtypeStruct((GROUP, 3 * TILE, DIM), BF16),
        scratch_shapes=[turned(), acc(), acc()],
        compiler_params=params(),
        cost_estimate=pl.CostEstimate(flops=OWN_FLOPS, bytes_accessed=2**22, transcendentals=0),
        name="own_row",
    )(qd, own, e, share, dqt)


def per_device(queries, keys, values, d_out, saved_out, mask):
    group = ("frame", "head")
    row = lax.axis_index("row")
    is_even = lax.rem(row, 2) == 0
    chip_swap = [(i, i ^ 1) for i in range(ROWS)]
    link_swap = [(i, i + 1) for i in range(1, ROWS - 1, 2)] + [(i + 1, i) for i in range(1, ROWS - 1, 2)]

    def exchange(x):
        return lax.all_to_all(x, group, split_axis=0, concat_axis=0, tiled=True)

    w = lax.axis_index("head").astype(jnp.int32).reshape(1)
    own = exchange(pack_first(keys, values))
    second = pack_second(w, queries, d_out, saved_out, mask)
    own, second = lax.optimization_barrier((own, second))
    qd = exchange(second)
    far = lax.ppermute(own, "row", link_swap)
    near = lax.ppermute(own, "row", chip_swap)

    far_index = jnp.where(is_even, row - 1, row + 1)
    near_index = jnp.where(is_even, row + 1, row - 1)
    rows = jnp.stack([near_index, row, far_index]).astype(jnp.int32)
    inside = ((rows >= 0) & (rows < ROWS)).astype(jnp.int32)
    rows = jnp.concatenate([jnp.clip(rows, 0, ROWS - 1), inside])
    live = qd[:, 2 * TILE + 2 : 2 * TILE + 4, :].astype(jnp.int32).reshape(GROUP, 2 * TILE)

    e, peak, total = early(rows, live, qd, own, near)
    far_part, share, dqt = far_row(rows, live, qd, far, peak, total)
    far_back = lax.ppermute(far_part, "row", link_swap)
    near_part, dqt = near_row(qd, near, e, share, dqt)
    near_back = lax.ppermute(near_part, "row", chip_swap)
    mine = own_row(qd, own, e, share, dqt)
    return tuple(unpack(exchange(add_parts(mine, near_back, far_back))))


def solution(mesh):
    devices = mesh.devices
    if mesh.axis_names != ("head", "blk"):
        raise ValueError("mesh axes")
    heads = devices.shape[0]
    grid = Mesh(devices.reshape(heads, FRAMES, devices.shape[1] // FRAMES), ("head", "frame", "row"))
    tokens = P(("frame", "row", "head"), None)
    return jax.shard_map(
        per_device,
        mesh=grid,
        in_specs=(tokens,) * 5 + (P(("frame", "row"), None),),
        out_specs=(tokens,) * 3,
        check_vma=False,
    )
```
